128 devices in a mesh: section: 8 (over x, core), expert: 16 (over z, y).
Axes of the slice: x: 4, y: 4, z: 4, core: 2. Of those that a mesh axis runs over, the one named last changes fastest.
Arguments:
- inputs: bfloat16 [8, 2, 1024, 2048], P('section', None, 'expert'), may hold values from -6 to 6
- routes: int32 [8, 2, 1024, 10], P('section', None, 'expert'), may hold values from 0 to 15, all different within a row; in each aligned block of 64 rows (0 to 63, 64 to 127, ..., all dimensions but the last counted through in order) at most 48 rows name the same one
- gates: float32 [8, 2, 1024, 10], P('section', None, 'expert'), may hold values from 0.1 to 0.6
- cot_early: bfloat16 [8, 1024, 2048], P('section', 'expert'), may hold values from -6 to 6
- head_grad: bfloat16 [1024, 2048], P('expert'), may hold values from -6 to 6
- w_gate: bfloat16 [8, 16, 2048, 512], P('section', 'expert'), may hold values from -0.125 to 0.125
- w_up: bfloat16 [8, 16, 2048, 512], P('section', 'expert'), may hold values from -0.125 to 0.125
- w_down: bfloat16 [8, 16, 512, 2048], P('section', 'expert'), may hold values from -0.25 to 0.25
Outputs:
- grad_early: bfloat16 [8, 1024, 2048], P('section', 'expert')
- grad_late: bfloat16 [8, 1024, 2048], P('section', 'expert')
- grad_gate: bfloat16 [8, 16, 2048, 512], P('section', 'expert')
- grad_up: bfloat16 [8, 16, 2048, 512], P('section', 'expert')
- grad_down: bfloat16 [8, 16, 512, 2048], P('section', 'expert')
The draws below stay inside these ranges and needn't reach their ends.
Inputs may be any that keep to these rules, and one draw needn't show every extreme that they name: `routes`: each row names 10 different experts. In each aligned block of 64 rows (one device's tokens of one micro-batch at one section) no expert is named by more than 48 rows, a bound that some block reaches.
All inputs are finite; a program needn't handle non-finite values.
Results may differ from the reference program's by a relative error of at most 0.008.
Values may be sent and summed in bfloat16 or wider, within the bound.
A program may use at most 128 MiB of HBM per device.

```python
import math
import jax
import jax.numpy as jnp
import numpy as np
from jax import lax

D = 2048
FF_E = 512
TOPK = 10
EXPERTS = 16
TOK_DEV = 64
CAP = 48
TOKENS = 1024
SECTIONS = 8
N_EXPERT = 16


def steps_of(rng, shape, cuts, smallest, high):
    loudness, own = 1.0, jax.random.fold_in(rng, 6)
    for axis_at, parts in cuts:
        draws = jnp.exp(jax.random.uniform(jax.random.fold_in(own, axis_at), (parts,), jnp.float32, smallest / len(cuts), high / len(cuts)))
        loudness = loudness * jnp.repeat(draws, shape[axis_at] // parts).reshape([-1 if axis == axis_at else 1 for axis in range(len(shape))])
    return loudness


def assign_block(rng, own, number, rows, number_of, top, limit, lean):
    order = jax.random.permutation(rng, number_of)
    crowded, usual = shares(number_of, rows * top, limit, lean, True), shares(number_of, rows * top, limit, lean, False)
    places = jnp.arange(number_of)

    def named(tallies, offset_by):
        used = int((tallies > 0).sum())
        fixed = max(1, used // 4)
        passed = fixed + (places - fixed + offset_by * (used - fixed)) % max(1, number_of - fixed)
        return jnp.zeros((number_of,), jnp.int32).at[order[jnp.where(places < fixed, places, passed)]].set(jnp.asarray(tallies, jnp.int32))

    tallies = jnp.where(number % 4 == 0, named(crowded, number // 4), named(usual, number - number // 4 - 1))
    mixed = jax.random.permutation(jax.random.fold_in(own, 3), number_of)
    donor, sink = mixed[0:number_of // 2 * 2:2], mixed[1:number_of // 2 * 2:2]
    margin = jnp.minimum(tallies[donor] - 1, limit - tallies[sink]) // 2
    margin = jnp.where((donor == order[0]) | (sink == order[0]) | (tallies[sink] == 0), 0, jnp.maximum(margin, 0))
    passed = jax.random.randint(jax.random.fold_in(own, 4), (number_of // 2,), 0, 1 << 20) % (margin + 1)
    tallies = tallies.at[donor].add(-passed).at[sink].add(passed)
    members = jnp.searchsorted(jnp.cumsum(tallies), jnp.arange(rows * top), side="right").astype(jnp.int32)
    table = members.reshape(top, rows).T
    table = table[jax.random.permutation(jax.random.fold_in(own, 1), rows)]
    offset_by = jax.random.randint(jax.random.fold_in(own, 2), (rows, 1), 0, top)
    return jnp.take_along_axis(table, (jnp.arange(top)[None, :] + offset_by) % top, axis=1)


def shares(count, total, bound, skew, full):
    weights = [(1 << 20) // math.isqrt(standing ** skew) + 1 for standing in range(1, count + 1)]
    largest = bound if full else min(bound, max(-(-total // count), total * weights[0] // sum(weights)))
    least = 1 if total - largest >= count - 1 else 0
    holding, rest = [largest] + [least] * (count - 1), total - largest - least * (count - 1)
    while rest > 0:
        movable = [i for i in range(1, count) if holding[i] < largest] or [i for i in range(1, count) if holding[i] < bound]
        whole, left = sum([weights[i] for i in movable]), rest
        for i in movable:
            addition = min(bound - holding[i], max(1, left * weights[i] // whole), rest)
            holding[i] = holding[i] + addition
            rest = rest - addition
    return np.array(holding)


def normal_values(key, extent, scale, most, shards=(), kind=jnp.bfloat16):
    loudness = steps_of(key, extent, shards, -0.22, 0.18) if shards else 1.0
    values = jax.random.normal(key, extent, jnp.float32) * scale * loudness
    return jnp.minimum(jnp.maximum(values, -most), most).astype(kind)


def setup_inputs(seed: int = 0) -> dict:
    keys = jax.random.split(jax.random.key(seed), 9)
    inputs = normal_values(keys[0], (SECTIONS, 2, TOKENS, D), 1.0, 6.0, ((0, 8), (2, 16)))
    routes_keys = jax.random.split(jax.random.fold_in(keys[1], 1), SECTIONS * 2 * TOKENS // TOK_DEV)
    routes_turns = jax.random.permutation(jax.random.fold_in(keys[1], 3), SECTIONS * 2 * TOKENS // TOK_DEV)
    routes = jax.vmap(lambda own, number: assign_block(jax.random.fold_in(keys[1], 2), own, number, TOK_DEV, EXPERTS, TOPK, CAP, 2))(routes_keys, routes_turns).reshape((SECTIONS, 2, TOKENS, TOPK))
    gates = jnp.clip(0.1 + 0.5 * jax.random.uniform(keys[2], (SECTIONS, 2, TOKENS, TOPK), jnp.float32) ** steps_of(keys[2], (SECTIONS, 2, TOKENS, TOPK), ((0, 8), (2, 16)), -0.2, 0.2), 0.1, 0.6)
    cot_early = normal_values(keys[3], (SECTIONS, TOKENS, D), 1.0, 6.0, ((0, 8), (1, 16)))
    head_grad = normal_values(keys[4], (TOKENS, D), 1.0, 6.0, ((0, 16),))
    w_gate = normal_values(keys[5], (SECTIONS, EXPERTS, D, FF_E), D ** -0.5, 0.125, ((0, 8), (1, 16)))
    w_up = normal_values(keys[6], (SECTIONS, EXPERTS, D, FF_E), D ** -0.5, 0.125, ((0, 8), (1, 16)))
    w_down = normal_values(keys[7], (SECTIONS, EXPERTS, FF_E, D), FF_E ** -0.5, 0.25, ((0, 8), (1, 16)))
    return {"inputs": inputs, "routes": routes, "gates": gates, "cot_early": cot_early, "head_grad": head_grad, "w_gate": w_gate, "w_up": w_up, "w_down": w_down}


def swish_parts(gate_value):
    sigmoid_value = jax.nn.sigmoid(gate_value)
    swished = gate_value * sigmoid_value
    derivative = sigmoid_value * (1.0 + gate_value * (1.0 - sigmoid_value))
    return swished, derivative


def expert_backward(row_inputs, row_grads, weight_gate, weight_up, weight_down, with_terms):
    gate_value = jnp.dot(row_inputs, weight_gate, preferred_element_type=jnp.float32)
    up_value = jnp.dot(row_inputs, weight_up, preferred_element_type=jnp.float32)
    swished, derivative = swish_parts(gate_value)
    grad_hidden = jnp.dot(row_grads, weight_down.T, preferred_element_type=jnp.float32)
    grad_gate_value = (grad_hidden * up_value * derivative).astype(jnp.bfloat16)
    grad_up_value = (grad_hidden * swished).astype(jnp.bfloat16)
    back_rows = (jnp.dot(grad_gate_value, weight_gate.T, preferred_element_type=jnp.float32)
                 + jnp.dot(grad_up_value, weight_up.T, preferred_element_type=jnp.float32)).astype(jnp.bfloat16)
    if not with_terms:
        return back_rows, ()
    hidden = (swished * up_value).astype(jnp.bfloat16)
    term_gate = jnp.dot(row_inputs.T, grad_gate_value, preferred_element_type=jnp.float32)
    term_up = jnp.dot(row_inputs.T, grad_up_value, preferred_element_type=jnp.float32)
    term_down = jnp.dot(hidden.T, row_grads, preferred_element_type=jnp.float32)
    return back_rows, (term_gate, term_up, term_down)


def layer_backward(tokens_in, route_ids, gate_weights, cotangent, weight_gate, weight_up, weight_down, with_terms):
    scaled = (gate_weights[:, :, None] * cotangent[:, None, :].astype(jnp.float32)).astype(jnp.bfloat16)
    scaled = scaled.reshape(TOKENS * TOPK, D)
    flat_ids = route_ids.reshape(-1)
    capacity = N_EXPERT * CAP

    def per_expert(summed, operands):
        expert_id, expert_gate, expert_up, expert_down = operands
        chosen = flat_ids == expert_id
        picked = jnp.argsort(jnp.where(chosen, 0, 1), stable=True)[:capacity].astype(jnp.int32)
        present = chosen[picked][:, None]
        row_inputs = jnp.where(present, tokens_in[picked // TOPK], jnp.zeros((), tokens_in.dtype))
        row_grads = jnp.where(present, scaled[picked], jnp.zeros((), scaled.dtype))
        back_rows, terms = expert_backward(row_inputs, row_grads, expert_gate, expert_up, expert_down, with_terms)
        summed = summed.at[picked].add(jnp.where(present, back_rows.astype(jnp.float32), jnp.zeros((), jnp.float32)))
        return summed, terms

    start = jnp.zeros((TOKENS * TOPK, D), jnp.float32)
    expert_ids = jnp.arange(EXPERTS, dtype=jnp.int32)
    summed, terms = lax.scan(per_expert, start, (expert_ids, weight_gate, weight_up, weight_down))
    result = cotangent.astype(jnp.float32) + jnp.sum(summed.reshape(TOKENS, TOPK, D), axis=1)
    return result.astype(jnp.bfloat16), terms


def reference(inputs, routes, gates, cot_early, head_grad, w_gate, w_up, w_down):
    def early_section(operands):
        tokens_in, route_ids, gate_weights, cotangent, weight_gate, weight_up, weight_down = operands
        result, unused = layer_backward(tokens_in[0], route_ids[0], gate_weights[0], cotangent,
                                        weight_gate, weight_up, weight_down, False)
        return result

    grad_early = lax.map(early_section, (inputs, routes, gates, cot_early, w_gate, w_up, w_down))
    cot_late = jnp.concatenate([grad_early[1:], head_grad[None]], axis=0)

    def late_section(operands):
        tokens_in, route_ids, gate_weights, first_cot, second_cot, weight_gate, weight_up, weight_down = operands
        unused, terms_first = layer_backward(tokens_in[0], route_ids[0], gate_weights[0], first_cot,
                                             weight_gate, weight_up, weight_down, True)
        result, terms_second = layer_backward(tokens_in[1], route_ids[1], gate_weights[1], second_cot,
                                              weight_gate, weight_up, weight_down, True)
        sums = tuple((terms_first[index] + terms_second[index]).astype(jnp.bfloat16) for index in range(3))
        return result, sums

    grad_late, sums = lax.map(late_section, (inputs, routes, gates, cot_early, cot_late, w_gate, w_up, w_down))
    return grad_early, grad_late, sums[0], sums[1], sums[2]
```

```python
import jax
import jax.numpy as jnp
from jax import lax
from jax.sharding import PartitionSpec as P

F32 = jnp.float32
BF16 = jnp.bfloat16


def shifted(x, axis, by):
    peers = lax.axis_size(axis)
    pairs = [(i, i + by) for i in range(peers) if 0 <= i + by < peers]
    return lax.ppermute(x, axis, pairs)


def gather_rows(x):
    return lax.all_gather(x, "expert", axis=0, tiled=True)


def forward(rows, weight_gate, weight_up):
    gate_value = jnp.dot(rows, weight_gate, preferred_element_type=F32)
    up_value = jnp.dot(rows, weight_up, preferred_element_type=F32)
    return gate_value, up_value


def backward(values, scaled, weight_gate, weight_up, weight_down):
    gate_value, up_value = values
    sigmoid_value = jax.nn.sigmoid(gate_value)
    swished = gate_value * sigmoid_value
    derivative = sigmoid_value * (1.0 + gate_value * (1.0 - sigmoid_value))
    hidden = (swished * up_value).astype(BF16)
    grad_hidden = lax.dot_general(
        scaled, weight_down, (((1,), (1,)), ((), ())), preferred_element_type=F32
    )
    grad_gate_value = (grad_hidden * up_value * derivative).astype(BF16)
    grad_up_value = (grad_hidden * swished).astype(BF16)
    dims = (((1,), (1,)), ((), ()))
    back = lax.dot_general(grad_gate_value, weight_gate, dims, preferred_element_type=F32)
    back = back + lax.dot_general(grad_up_value, weight_up, dims, preferred_element_type=F32)
    return back.astype(BF16), (hidden, grad_gate_value, grad_up_value)


def outer(left, right):
    return lax.dot_general(left, right, (((0,), (0,)), ((), ())), preferred_element_type=F32)


def weight_terms(rows, scaled, saved):
    hidden, grad_gate_value, grad_up_value = saved
    return (outer(rows, grad_gate_value), outer(rows, grad_up_value), outer(hidden, scaled))


def on_device(inputs, routes, gates, cot_early, head_grad, w_gate, w_up, w_down):
    weight_gate, weight_up, weight_down = (w_gate[0, 0], w_up[0, 0], w_down[0, 0])
    owners = lax.axis_size("expert")
    me = lax.axis_index("expert")
    section_index = lax.axis_index("section")
    top_section = lax.axis_size("section") - 1
    ids = jnp.arange(owners, dtype=jnp.int32)
    chosen = routes[0][..., None] == ids
    dense = jnp.sum(jnp.where(chosen, gates[0][..., None], 0.0), axis=2)
    dense = lax.all_gather(dense, "expert", axis=1, tiled=True)
    own_gate = jnp.sum(jnp.where(ids == me, dense, 0.0), axis=2)[..., None]
    first_rows = gather_rows(inputs[0, 0])
    first_cot = gather_rows(cot_early[0])
    second_rows = gather_rows(inputs[0, 1])
    first_scaled = (own_gate[0] * first_cot.astype(F32)).astype(BF16)
    first_back, first_saved = backward(
        forward(first_rows, weight_gate, weight_up), first_scaled, weight_gate, weight_up, weight_down
    )
    summed = lax.psum_scatter(first_back, "expert", scatter_dimension=0, tiled=True)
    grad_early = (cot_early[0].astype(F32) + summed.astype(F32)).astype(BF16)
    received = shifted(grad_early, "section", -1)
    second_cot = jnp.where(section_index == top_section, head_grad, received)
    second_all = gather_rows(second_cot)
    second_scaled = (own_gate[1] * second_all.astype(F32)).astype(BF16)
    second_back, second_saved = backward(
        forward(second_rows, weight_gate, weight_up), second_scaled, weight_gate, weight_up, weight_down
    )
    summed = lax.psum_scatter(second_back, "expert", scatter_dimension=0, tiled=True)
    grad_late = (second_cot.astype(F32) + summed.astype(F32)).astype(BF16)
    first_terms = weight_terms(first_rows, first_scaled, first_saved)
    second_terms = weight_terms(second_rows, second_scaled, second_saved)
    grad_gate, grad_up, grad_down = (
        (a + b).astype(BF16)[None, None] for a, b in zip(first_terms, second_terms)
    )
    return grad_early[None], grad_late[None], grad_gate, grad_up, grad_down


def solution(mesh):
    in_specs = (
        P("section", None, "expert", None),
        P("section", None, "expert", None),
        P("section", None, "expert", None),
        P("section", "expert", None),
        P("expert", None),
        P("section", "expert", None, None),
        P("section", "expert", None, None),
        P("section", "expert", None, None),
    )
    out_specs = (
        P("section", "expert", None),
        P("section", "expert", None),
        P("section", "expert", None, None),
        P("section", "expert", None, None),
        P("section", "expert", None, None),
    )
    return jax.shard_map(
        on_device, mesh=mesh, in_specs=in_specs, out_specs=out_specs, check_vma=False
    )
```

```python
import functools

import jax
import jax.numpy as jnp
from jax import lax
from jax.experimental import pallas as pl
from jax.experimental.pallas import tpu as pltpu
from jax.sharding import PartitionSpec as P

F32 = jnp.float32
BF16 = jnp.bfloat16
MESH = pl.DeviceIdType.MESH

D = 2048
FF = 512
TOPK = 10
OWNERS = 16
SIDE = 4
ROWS = 16
CHUNKS = 4
STEPS = 2 * CHUNKS
WIDE = D + 128
HALF = D // 2
QUART = D // 4
COT_CUT = 1024
ALL_ROWS = OWNERS * ROWS
NT = (((1,), (1,)), ((), ()))
TN = (((0,), (0,)), ((), ()))


def kernel(
    inputs, routes, gates, cot_early, head_grad, w_gate, w_up, w_down,
    grads, grad_gate, grad_up, grad_down,
    xs, cots, part, land1z, land1y, land2z, land2y, land3, land4, moved, outs, head,
    wg, wu, wd, gate_s, up_s, hid_s, gg_s, gu_s, scaled_s, acc_g, acc_u, acc_d,
    load_sem, ag_send, ag_recv, rs_send, rs_recv, mv_send, mv_recv,
):
    sec = lax.axis_index("section")
    own = lax.axis_index("expert")
    n_sec = lax.axis_size("section")
    z = own // SIDE
    y = own % SIDE
    zp, zm, zo = (z + 1) % SIDE, (z + 3) % SIDE, (z + 2) % SIDE
    yp, ym, yo = (y + 1) % SIDE, (y + 3) % SIDE, (y + 2) % SIDE
    to_zp = (sec, zp * SIDE + y)
    to_zm = (sec, zm * SIDE + y)
    to_yp = (sec, z * SIDE + yp)
    to_ym = (sec, z * SIDE + ym)
    to_below = ((sec + n_sec - 1) % n_sec, own)
    to_above = ((sec + 1) % n_sec, own)

    def at_rows(i):
        return pl.ds(pl.multiple_of(i * ROWS, ROWS), ROWS)

    def blk(buf, k, bz, by, col, width):
        return buf.at[k, bz, at_rows(by), pl.ds(col, width)]

    def zrow(buf, k, bz, col, width):
        return buf.at[k, bz, :, pl.ds(col, width)]

    def ycol(buf, k, by, col, width):
        return buf.at[k, :, at_rows(by), pl.ds(col, width)]

    def remote(src, dst, send, recv, peer):
        return pltpu.make_async_remote_copy(
            src_ref=src, dst_ref=dst, send_sem=send, recv_sem=recv,
            device_id=peer, device_id_type=MESH,
        )

    def ag_copy(which, phase, side, k, arriving):
        buf = cots if which else xs
        width = WIDE if which else D
        cut = COT_CUT if which else HALF
        late = phase >= 2
        on_y = (phase < 2) != bool(which)
        here, plus, minus = (y, yp, ym) if on_y else (z, zp, zm)
        peer = ((to_yp, to_ym) if on_y else (to_zp, to_zm))[side]
        opposite = yo if on_y else zo
        if phase % 2 == 0:
            pos = ((minus, plus)[side]) if arriving else here
            col, wid = 0, width
        else:
            pos = opposite if arriving else (minus, plus)[side]
            col, wid = (0, cut) if side == 0 else (cut, width - cut)
        if late:
            ref = (ycol if on_y else zrow)(buf, k, pos, col, wid)
        elif on_y:
            ref = blk(buf, k, z, pos, col, wid)
        else:
            ref = blk(buf, k, pos, y, col, wid)
        slot = phase * 2 + side
        return remote(ref, ref, ag_send.at[k, which, slot], ag_recv.at[k, which, slot], peer)

    def ag_start(phase, k):
        for which in range(2):
            for side in range(2):
                ag_copy(which, phase, side, k, False).start()

    def ag_wait(phase, k):
        for which in range(2):
            for side in range(2):
                ag_copy(which, phase, side, k, True).wait_recv()

    def rs_copy(phase, part_no, side, k):
        on_y = (part_no == 1) != (phase >= 2)
        base = part_no * HALF
        plus, minus, opposite = (yp, ym, yo) if on_y else (zp, zm, zo)
        peer = ((to_ym, to_yp) if on_y else (to_zm, to_zp))[side]
        if phase % 2 == 0:
            pos = opposite
            col, wid = base + side * QUART, QUART
        else:
            pos = (minus, plus)[side]
            col, wid = base, HALF
        if phase < 2:
            src = (ycol if on_y else zrow)(part, k, pos, col, wid)
            lands = ((land1z, land2z), (land1y, land2y))[part_no]
            dst = lands[phase].at[k, side]
        else:
            src = blk(part, k, z, pos, col, wid) if on_y else blk(part, k, pos, y, col, wid)
            dst = (land3, land4)[phase - 2].at[k, part_no * 2 + side]
        slot = phase * 4 + part_no * 2 + side
        return remote(src, dst, rs_send.at[k, slot], rs_recv.at[k, slot], peer)

    def rs_start(phase, k):
        for part_no in range(2):
            for side in range(2):
                rs_copy(phase, part_no, side, k).start()

    def rs_wait(phase, k):
        for part_no in range(2):
            for side in range(2):
                rs_copy(phase, part_no, side, k).wait_recv()

    def add_to(ref, *others):
        total = ref[...].astype(F32)
        for other in others:
            total = total + other[...].astype(F32)
        ref[...] = total.astype(BF16)

    def move(c):
        return remote(outs.at[c], moved.at[c], mv_send.at[c], mv_recv.at[c], to_below)

    loads = [
        pltpu.make_async_copy(w_gate, wg, load_sem.at[0]),
        pltpu.make_async_copy(w_up, wu, load_sem.at[1]),
        pltpu.make_async_copy(w_down, wd, load_sem.at[2]),
        pltpu.make_async_copy(head_grad, head, load_sem.at[3]),
    ]

    def row_load(k):
        c = k % CHUNKS
        m = k // CHUNKS
        return pltpu.make_async_copy(
            inputs.at[m, pl.ds(c * ROWS, ROWS), :], blk(xs, k, z, y, 0, D), load_sem.at[4 + k]
        )

    def cot_load(c):
        return pltpu.make_async_copy(
            cot_early.at[pl.ds(c * ROWS, ROWS), :], blk(cots, c, z, y, 0, D), load_sem.at[4 + STEPS + c]
        )

    for c in range(CHUNKS):
        row_load(c).start()
        cot_load(c).start()
    for copy in loads:
        copy.start()
    for c in range(CHUNKS, STEPS):
        row_load(c).start()

    barrier = pltpu.get_barrier_semaphore()
    for peer in (to_yp, to_ym, to_zp, to_zm, to_below, to_above):
        pl.semaphore_signal(barrier, inc=1, device_id=peer, device_id_type=MESH)

    lane = lax.broadcasted_iota(jnp.int32, (ROWS, 128), 1)
    for k in range(STEPS):
        m, c = divmod(k, CHUNKS)
        ids = routes[m, c * ROWS:(c + 1) * ROWS, :]
        values = gates[m, c * ROWS:(c + 1) * ROWS, :]
        dense = jnp.zeros((ROWS, 128), F32)
        for choice in range(TOPK):
            hit = ids[:, choice:choice + 1] == (lane & (OWNERS - 1))
            dense = dense + jnp.where(hit, values[:, choice:choice + 1], 0.0)
        high = dense.astype(BF16).astype(F32)
        rest = dense - high
        mid = rest.astype(BF16).astype(F32)
        low = rest - mid
        packed = jnp.where(
            lane < OWNERS, high,
            jnp.where(lane < 2 * OWNERS, mid, jnp.where(lane < 3 * OWNERS, low, 0.0)),
        )
        blk(cots, k, z, y, D, 128)[...] = packed.astype(BF16)

    acc_g[...] = jnp.zeros_like(acc_g)
    acc_u[...] = jnp.zeros_like(acc_u)
    acc_d[...] = jnp.zeros_like(acc_d)
    pick_row = lax.broadcasted_iota(jnp.int32, (128, 128), 0)
    picker = jnp.where(
        ((pick_row & (OWNERS - 1)) == own) & (pick_row < 3 * OWNERS), 1.0, 0.0
    ).astype(BF16)

    for c in range(CHUNKS):
        row_load(c).wait()
        cot_load(c).wait()
    pl.semaphore_wait(barrier, 6)
    ag_start(0, 0)
    for copy in loads:
        copy.wait()
    for c in range(CHUNKS, STEPS):
        row_load(c).wait()
    ag_wait(0, 0)
    ag_start(1, 0)
    ag_wait(1, 0)
    ag_start(2, 0)

    def forward(j):
        rows = xs[j].reshape(ALL_ROWS, D)
        for n in range(2):
            cols = slice(n * 256, (n + 1) * 256)
            gate_s[:, cols] = jnp.dot(rows, wg[:, cols], preferred_element_type=F32)
            up_s[:, cols] = jnp.dot(rows, wu[:, cols], preferred_element_type=F32)

    def backward(j):
        turn = j % 2
        own_gate = jnp.dot(
            cots[j, :, :, D:].reshape(ALL_ROWS, 128), picker, preferred_element_type=F32
        )
        for n in range(D // 128):
            cols = slice(n * 128, (n + 1) * 128)
            tile = cots[j, :, :, cols].reshape(ALL_ROWS, 128).astype(F32)
            scaled_s[turn, :, cols] = (own_gate * tile).astype(BF16)
        for n in range(2):
            cols = slice(n * 256, (n + 1) * 256)
            grad_hidden = lax.dot_general(
                scaled_s[turn], wd[cols, :], NT, preferred_element_type=F32
            )
            gate_value = gate_s[:, cols]
            up_value = up_s[:, cols]
            sigmoid_value = jax.nn.sigmoid(gate_value)
            swished = gate_value * sigmoid_value
            derivative = sigmoid_value * (1.0 + gate_value * (1.0 - sigmoid_value))
            hid_s[turn, :, cols] = (swished * up_value).astype(BF16)
            gg_s[turn, :, cols] = (grad_hidden * up_value * derivative).astype(BF16)
            gu_s[turn, :, cols] = (grad_hidden * swished).astype(BF16)
        for n in range(D // 256):
            cols = slice(n * 256, (n + 1) * 256)
            back = lax.dot_general(gg_s[turn], wg[cols, :], NT, preferred_element_type=F32)
            back = back + lax.dot_general(gu_s[turn], wu[cols, :], NT, preferred_element_type=F32)
            part[j, :, :, cols] = back.astype(BF16).reshape(SIDE, SIDE * ROWS, 256)

    def grow_up_gate(r):
        turn = r % 2
        for n in range(D // 256):
            cols = slice(n * 256, (n + 1) * 256)
            rows = xs[r, :, :, cols].reshape(ALL_ROWS, 256)
            acc_g[cols, :] += lax.dot_general(rows, gg_s[turn], TN, preferred_element_type=F32)
            acc_u[cols, :] += lax.dot_general(rows, gu_s[turn], TN, preferred_element_type=F32)

    def grow_down(r):
        turn = r % 2
        for n in range(D // 256):
            cols = slice(n * 256, (n + 1) * 256)
            acc_d[:, cols] += lax.dot_general(
                hid_s[turn], scaled_s[turn, :, cols], TN, preferred_element_type=F32
            )

    @pl.loop(0, STEPS + 2)
    def _(t):
        k, j, r, n = t, t - 1, t - 2, t + 1
        gathering = k < STEPS
        coming = n < STEPS
        working = (t >= 1) & (j < STEPS)
        reducing = t >= 2

        @pl.when(reducing)
        def _():
            rs_wait(0, r)
            add_to(zrow(part, r, zm, 0, QUART), land1z.at[r, 0])
            add_to(zrow(part, r, zp, QUART, QUART), land1z.at[r, 1])
            add_to(ycol(part, r, ym, HALF, QUART), land1y.at[r, 0])
            add_to(ycol(part, r, yp, HALF + QUART, QUART), land1y.at[r, 1])
            rs_start(1, r)

        @pl.when(working)
        def _():
            forward(j)

        @pl.when(coming & (n >= CHUNKS))
        def _():
            c = n - CHUNKS
            move(c).wait_recv()
            top = sec == n_sec - 1
            value = jnp.where(top, head[at_rows(c), :], moved[c])
            blk(cots, n, z, y, 0, D)[...] = value

        @pl.when(coming)
        def _():
            ag_start(0, n)

        @pl.when(working)
        def _():
            backward(j)
            rs_start(0, j)

        @pl.when(gathering)
        def _():
            ag_wait(2, k)
            ag_start(3, k)

        @pl.when(reducing)
        def _():
            rs_wait(1, r)
            add_to(zrow(part, r, z, 0, HALF), land2z.at[r, 0], land2z.at[r, 1])
            add_to(ycol(part, r, y, HALF, HALF), land2y.at[r, 0], land2y.at[r, 1])
            rs_start(2, r)
            grow_up_gate(r)

        @pl.when(coming)
        def _():
            ag_wait(0, n)
            ag_start(1, n)

        @pl.when(reducing)
        def _():
            rs_wait(2, r)
            add_to(blk(part, r, z, ym, 0, QUART), land3.at[r, 0])
            add_to(blk(part, r, z, yp, QUART, QUART), land3.at[r, 1])
            add_to(blk(part, r, zm, y, HALF, QUART), land3.at[r, 2])
            add_to(blk(part, r, zp, y, HALF + QUART, QUART), land3.at[r, 3])
            rs_start(3, r)
            grow_down(r)

        @pl.when(coming)
        def _():
            ag_wait(1, n)
            ag_start(2, n)

        @pl.when(reducing)
        def _():
            rs_wait(3, r)
            for part_no in range(2):
                base = part_no * HALF
                total = blk(cots, r, z, y, base, HALF)[...].astype(F32)
                total = total + blk(part, r, z, y, base, HALF)[...].astype(F32)
                total = total + land4[r, part_no * 2].astype(F32)
                total = total + land4[r, part_no * 2 + 1].astype(F32)
                outs[r, :, base:base + HALF] = total.astype(BF16)

            @pl.when(r < CHUNKS)
            def _():
                move(r).start()

        @pl.when(gathering)
        def _():
            ag_wait(3, k)

    wg[...] = acc_g[...].astype(BF16)
    store_g = pltpu.make_async_copy(wg, grad_gate, load_sem.at[0])
    store_g.start()
    wu[...] = acc_u[...].astype(BF16)
    store_u = pltpu.make_async_copy(wu, grad_up, load_sem.at[1])
    store_u.start()
    wd[...] = acc_d[...].astype(BF16)
    store_d = pltpu.make_async_copy(wd, grad_down, load_sem.at[2])
    store_d.start()
    store_o = pltpu.make_async_copy(outs, grads, load_sem.at[3])
    store_o.start()

    @pl.loop(0, STEPS)
    def _(k):
        for phase in range(4):
            for which in range(2):
                for side in range(2):
                    ag_copy(which, phase, side, k, False).wait_send()
                    rs_copy(phase, which, side, k).wait_send()

    @pl.loop(0, CHUNKS)
    def _(c):
        move(c).wait_send()

    for copy in (store_g, store_u, store_d, store_o):
        copy.wait()


def on_device(inputs, routes, gates, cot_early, head_grad, w_gate, w_up, w_down):
    hbm = pl.BlockSpec(memory_space=pl.ANY)
    vmem = pl.BlockSpec(memory_space=pltpu.VMEM)
    shape = jax.ShapeDtypeStruct
    block = SIDE * ROWS
    grads, grad_gate, grad_up, grad_down = pl.pallas_call(
        kernel,
        out_shape=(
            shape((STEPS, ROWS, D), BF16),
            shape((D, FF), BF16),
            shape((D, FF), BF16),
            shape((FF, D), BF16),
        ),
        in_specs=[hbm, vmem, vmem, hbm, hbm, hbm, hbm, hbm],
        out_specs=[hbm] * 4,
        scratch_shapes=[
            pltpu.VMEM((STEPS, SIDE, block, D), BF16),
            pltpu.VMEM((STEPS, SIDE, block, WIDE), BF16),
            pltpu.VMEM((STEPS, SIDE, block, D), BF16),
            pltpu.VMEM((STEPS, 2, block, QUART), BF16),
            pltpu.VMEM((STEPS, 2, SIDE, ROWS, QUART), BF16),
            pltpu.VMEM((STEPS, 2, block, HALF), BF16),
            pltpu.VMEM((STEPS, 2, SIDE, ROWS, HALF), BF16),
            pltpu.VMEM((STEPS, 4, ROWS, QUART), BF16),
            pltpu.VMEM((STEPS, 4, ROWS, HALF), BF16),
            pltpu.VMEM((CHUNKS, ROWS, D), BF16),
            pltpu.VMEM((STEPS, ROWS, D), BF16),
            pltpu.VMEM((CHUNKS * ROWS, D), BF16),
            pltpu.VMEM((D, FF), BF16),
            pltpu.VMEM((D, FF), BF16),
            pltpu.VMEM((FF, D), BF16),
            pltpu.VMEM((ALL_ROWS, FF), F32),
            pltpu.VMEM((ALL_ROWS, FF), F32),
            pltpu.VMEM((2, ALL_ROWS, FF), BF16),
            pltpu.VMEM((2, ALL_ROWS, FF), BF16),
            pltpu.VMEM((2, ALL_ROWS, FF), BF16),
            pltpu.VMEM((2, ALL_ROWS, D), BF16),
            pltpu.VMEM((D, FF), F32),
            pltpu.VMEM((D, FF), F32),
            pltpu.VMEM((FF, D), F32),
            pltpu.SemaphoreType.DMA((4 + STEPS + CHUNKS,)),
            pltpu.SemaphoreType.DMA((STEPS, 2, 8)),
            pltpu.SemaphoreType.DMA((STEPS, 2, 8)),
            pltpu.SemaphoreType.DMA((STEPS, 16)),
            pltpu.SemaphoreType.DMA((STEPS, 16)),
            pltpu.SemaphoreType.DMA((CHUNKS,)),
            pltpu.SemaphoreType.DMA((CHUNKS,)),
        ],
        compiler_params=pltpu.CompilerParams(
            collective_id=0, has_side_effects=True, vmem_limit_bytes=67043328
        ),
        cost_estimate=pl.CostEstimate(
            flops=16 * 2 * 1024 * D * FF, bytes_accessed=16 << 20, transcendentals=2 * 1024 * FF
        ),
    )(inputs[0], routes[0], gates[0], cot_early[0], head_grad, w_gate[0, 0], w_up[0, 0], w_down[0, 0])
    tokens = CHUNKS * ROWS
    grads = grads.reshape(2, 1, tokens, D)
    return grads[0], grads[1], grad_gate[None, None], grad_up[None, None], grad_down[None, None]


def solution(mesh):
    in_specs = (
        P("section", None, "expert", None),
        P("section", None, "expert", None),
        P("section", None, "expert", None),
        P("section", "expert", None),
        P("expert", None),
        P("section", "expert", None, None),
        P("section", "expert", None, None),
        P("section", "expert", None, None),
    )
    out_specs = (
        P("section", "expert", None),
        P("section", "expert", None),
        P("section", "expert", None, None),
        P("section", "expert", None, None),
        P("section", "expert", None, None),
    )
    return jax.shard_map(
        on_device, mesh=mesh, in_specs=in_specs, out_specs=out_specs, check_vma=False
    )
```

```python
import functools

import jax
import jax.numpy as jnp
from jax import lax
from jax.experimental import pallas as pl
from jax.experimental.pallas import tpu as pltpu
from jax.sharding import PartitionSpec as P

F32 = jnp.float32
BF16 = jnp.bfloat16
MESH = pl.DeviceIdType.MESH

D = 2048
FF = 512
TOPK = 10
OWNERS = 16
SIDE = 4
ROWS = 16
CHUNKS = 4
STEPS = 2 * CHUNKS
WIDE = D + 128
HALF = D // 2
QUART = D // 4
COT_CUT = 1024
ALL_ROWS = OWNERS * ROWS
NT = (((1,), (1,)), ((), ()))
TN = (((0,), (0,)), ((), ()))
HEAD = (("P1", 0), ("P1", 1), ("P1", 2), ("P2", 0), ("P1", 3), ("P2", 1), ("P2", 2), ("P3", 0), ("P2", 3),
        ("P3", 1), ("P4", 0), ("P3", 2), ("P4", 1),)
AFTER = {
    (0, "H"): (("P3", 3), ("P4", 2),),
    (1, "W"): (("R1", 0), ("P4", 3),),
    (2, "G"): (("R1", 1), ("R2", 0),),
    (2, "W"): (("R1", 2),),
    (3, "F"): (("R2", 1),),
    (3, "G"): (("R3", 0),),
    (3, "H"): (("R1", 3), ("R2", 2),),
    (3, "W"): (("R4", 0), ("R3", 1), ("R2", 3), ("R3", 2), ("M", 0), ("R4", 1), ("P1", 4), ("R3", 3), ("R4",
        2), ("M", 1), ("P2", 4), ("R4", 3), ("M", 2), ("P1", 5), ("P3", 4), ("M", 3), ("P2", 5), ("P1", 6),
        ("P1", 7), ("P4", 4), ("P2", 6), ("P3", 5), ("P2", 7),),
    (4, "H"): (("P3", 6),),
    (4, "W"): (("P4", 5), ("P3", 7), ("P4", 6),),
    (5, "W"): (("R1", 4), ("P4", 7),),
    (6, "G"): (("R1", 5), ("R2", 4),),
    (6, "W"): (("R1", 6),),
    (7, "F"): (("R2", 5),),
    (7, "H"): (("R1", 7), ("R2", 6),),
    (8, "V"): (("R2", 7),),
    (8, "W"): (("R3", 4), ("R3", 5), ("R3", 6), ("R3", 7), ("R4", 4), ("R4", 5), ("R4", 6), ("R4", 7), ("M",
        4), ("M", 5), ("M", 6), ("M", 7),),
}


def kernel(
    inputs, routes, gates, cot_early, head_grad, w_gate, w_up, w_down,
    grads, grad_gate, grad_up, grad_down,
    xs, cots, part, land1z, land1y, land2z, land2y, land3, land4, moved, outs, head,
    wg, wu, wd, gate_s, up_s, hid_s, gg_s, gu_s, scaled_s, acc_g, acc_u, acc_d,
    load_sem, ag_send, ag_recv, rs_send, rs_recv, mv_send, mv_recv,
):
    sec = lax.axis_index("section")
    own = lax.axis_index("expert")
    n_sec = lax.axis_size("section")
    z = own // SIDE
    y = own % SIDE
    zp, zm, zo = (z + 1) % SIDE, (z + 3) % SIDE, (z + 2) % SIDE
    yp, ym, yo = (y + 1) % SIDE, (y + 3) % SIDE, (y + 2) % SIDE
    to_zp = (sec, zp * SIDE + y)
    to_zm = (sec, zm * SIDE + y)
    to_yp = (sec, z * SIDE + yp)
    to_ym = (sec, z * SIDE + ym)
    to_below = ((sec + n_sec - 1) % n_sec, own)
    to_above = ((sec + 1) % n_sec, own)

    def at_rows(i):
        return pl.ds(pl.multiple_of(i * ROWS, ROWS), ROWS)

    def blk(buf, k, bz, by, col, width):
        return buf.at[k, bz, at_rows(by), pl.ds(col, width)]

    def zrow(buf, k, bz, col, width):
        return buf.at[k, bz, :, pl.ds(col, width)]

    def ycol(buf, k, by, col, width):
        return buf.at[k, :, at_rows(by), pl.ds(col, width)]

    def remote(src, dst, send, recv, peer):
        return pltpu.make_async_remote_copy(
            src_ref=src, dst_ref=dst, send_sem=send, recv_sem=recv,
            device_id=peer, device_id_type=MESH,
        )

    def ag_copy(which, phase, side, k, arriving):
        buf = cots if which else xs
        width = WIDE if which else D
        cut = COT_CUT if which else HALF
        late = phase >= 2
        on_y = (phase < 2) != bool(which)
        here, plus, minus = (y, yp, ym) if on_y else (z, zp, zm)
        peer = ((to_yp, to_ym) if on_y else (to_zp, to_zm))[side]
        opposite = yo if on_y else zo
        if phase % 2 == 0:
            pos = ((minus, plus)[side]) if arriving else here
            col, wid = 0, width
        else:
            pos = opposite if arriving else (minus, plus)[side]
            col, wid = (0, cut) if side == 0 else (cut, width - cut)
        if late:
            ref = (ycol if on_y else zrow)(buf, k, pos, col, wid)
        elif on_y:
            ref = blk(buf, k, z, pos, col, wid)
        else:
            ref = blk(buf, k, pos, y, col, wid)
        slot = phase * 2 + side
        return remote(ref, ref, ag_send.at[k, which, slot], ag_recv.at[k, which, slot], peer)

    def ag_start(phase, k):
        for which in range(2):
            for side in range(2):
                ag_copy(which, phase, side, k, False).start()

    def ag_wait(phase, k):
        for which in range(2):
            for side in range(2):
                ag_copy(which, phase, side, k, True).wait_recv()

    def rs_copy(phase, part_no, side, k):
        on_y = (part_no == 1) != (phase >= 2)
        base = part_no * HALF
        plus, minus, opposite = (yp, ym, yo) if on_y else (zp, zm, zo)
        peer = ((to_ym, to_yp) if on_y else (to_zm, to_zp))[side]
        if phase % 2 == 0:
            pos = opposite
            col, wid = base + side * QUART, QUART
        else:
            pos = (minus, plus)[side]
            col, wid = base, HALF
        if phase < 2:
            src = (ycol if on_y else zrow)(part, k, pos, col, wid)
            lands = ((land1z, land2z), (land1y, land2y))[part_no]
            dst = lands[phase].at[k, side]
        else:
            src = blk(part, k, z, pos, col, wid) if on_y else blk(part, k, pos, y, col, wid)
            dst = (land3, land4)[phase - 2].at[k, part_no * 2 + side]
        slot = phase * 4 + part_no * 2 + side
        return remote(src, dst, rs_send.at[k, slot], rs_recv.at[k, slot], peer)

    def rs_start(phase, k):
        for part_no in range(2):
            for side in range(2):
                rs_copy(phase, part_no, side, k).start()

    def rs_wait(phase, k):
        for part_no in range(2):
            for side in range(2):
                rs_copy(phase, part_no, side, k).wait_recv()

    def add_to(ref, *others):
        total = ref[...].astype(F32)
        for other in others:
            total = total + other[...].astype(F32)
        ref[...] = total.astype(BF16)

    def move(c):
        return remote(outs.at[c], moved.at[c], mv_send.at[c], mv_recv.at[c], to_below)

    loads = [
        pltpu.make_async_copy(w_gate, wg, load_sem.at[0]),
        pltpu.make_async_copy(w_up, wu, load_sem.at[1]),
        pltpu.make_async_copy(w_down, wd, load_sem.at[2]),
        pltpu.make_async_copy(head_grad, head, load_sem.at[3]),
    ]

    def row_load(k):
        c = k % CHUNKS
        m = k // CHUNKS
        return pltpu.make_async_copy(
            inputs.at[m, pl.ds(c * ROWS, ROWS), :], blk(xs, k, z, y, 0, D), load_sem.at[4 + k]
        )

    def cot_load(c):
        return pltpu.make_async_copy(
            cot_early.at[pl.ds(c * ROWS, ROWS), :], blk(cots, c, z, y, 0, D), load_sem.at[4 + STEPS + c]
        )

    for c in range(CHUNKS):
        row_load(c).start()
        cot_load(c).start()
    for copy in loads:
        copy.start()
    for c in range(CHUNKS, STEPS):
        row_load(c).start()

    barrier = pltpu.get_barrier_semaphore()
    for peer in (to_yp, to_ym, to_zp, to_zm, to_below, to_above):
        pl.semaphore_signal(barrier, inc=1, device_id=peer, device_id_type=MESH)

    expert = lax.broadcasted_iota(jnp.int32, (OWNERS, CHUNKS * ROWS), 0)
    halves = []
    for m in range(2):
        dense = jnp.zeros((OWNERS, CHUNKS * ROWS), F32)
        for choice in range(TOPK):
            hit = routes[choice, m:m + 1, :] == expert
            dense = dense + jnp.where(hit, gates[choice, m:m + 1, :], 0.0)
        halves.append(dense)
    dense = jnp.concatenate(halves, axis=1)
    high = dense.astype(BF16).astype(F32)
    mid = (dense - high).astype(BF16).astype(F32)
    low = dense - high - mid
    blank = jnp.zeros((128 - 3 * OWNERS, STEPS * ROWS), F32)
    packed = jnp.concatenate([high, mid, low, blank], axis=0).T.astype(BF16)
    for k in range(STEPS):
        blk(cots, k, z, y, D, 128)[...] = packed[k * ROWS:(k + 1) * ROWS]

    pick_row = lax.broadcasted_iota(jnp.int32, (128, 128), 0)
    picker = jnp.where(
        ((pick_row & (OWNERS - 1)) == own) & (pick_row < 3 * OWNERS), 1.0, 0.0
    ).astype(BF16)

    def forward(j):
        rows = xs[j].reshape(ALL_ROWS, D)
        for n in range(2):
            cols = slice(n * 256, (n + 1) * 256)
            gate_s[:, cols] = jnp.dot(rows, wg[:, cols], preferred_element_type=F32)
            up_s[:, cols] = jnp.dot(rows, wu[:, cols], preferred_element_type=F32)

    def backward(j):
        turn = j % 2
        own_gate = jnp.dot(
            cots[j, :, :, D:].reshape(ALL_ROWS, 128), picker, preferred_element_type=F32
        )
        for n in range(D // 128):
            cols = slice(n * 128, (n + 1) * 128)
            tile = cots[j, :, :, cols].reshape(ALL_ROWS, 128).astype(F32)
            scaled_s[turn, :, cols] = (own_gate * tile).astype(BF16)
        for n in range(2):
            cols = slice(n * 256, (n + 1) * 256)
            grad_hidden = lax.dot_general(
                scaled_s[turn], wd[cols, :], NT, preferred_element_type=F32
            )
            gate_value = gate_s[:, cols]
            up_value = up_s[:, cols]
            sigmoid_value = jax.nn.sigmoid(gate_value)
            swished = gate_value * sigmoid_value
            derivative = sigmoid_value * (1.0 + gate_value * (1.0 - sigmoid_value))
            hid_s[turn, :, cols] = (swished * up_value).astype(BF16)
            gg_s[turn, :, cols] = (grad_hidden * up_value * derivative).astype(BF16)
            gu_s[turn, :, cols] = (grad_hidden * swished).astype(BF16)
    def send_back(j):
        turn = j % 2
        for n in range(D // 256):
            cols = slice(n * 256, (n + 1) * 256)
            back = lax.dot_general(gg_s[turn], wg[cols, :], NT, preferred_element_type=F32)
            back = back + lax.dot_general(gu_s[turn], wu[cols, :], NT, preferred_element_type=F32)
            part[j, :, :, cols] = back.astype(BF16).reshape(SIDE, SIDE * ROWS, 256)

    def grow_up_gate(r):
        turn = r % 2
        for n in range(D // 256):
            cols = slice(n * 256, (n + 1) * 256)
            rows = xs[r, :, :, cols].reshape(ALL_ROWS, 256)
            acc_g[cols, :] += lax.dot_general(rows, gg_s[turn], TN, preferred_element_type=F32)
            acc_u[cols, :] += lax.dot_general(rows, gu_s[turn], TN, preferred_element_type=F32)

    def grow_down(r):
        turn = r % 2
        for n in range(D // 256):
            cols = slice(n * 256, (n + 1) * 256)
            acc_d[:, cols] += lax.dot_general(
                hid_s[turn], scaled_s[turn, :, cols], TN, preferred_element_type=F32
            )

    def fold_far(r):
        add_to(zrow(part, r, zm, 0, QUART), land1z.at[r, 0])
        add_to(zrow(part, r, zp, QUART, QUART), land1z.at[r, 1])
        add_to(ycol(part, r, ym, HALF, QUART), land1y.at[r, 0])
        add_to(ycol(part, r, yp, HALF + QUART, QUART), land1y.at[r, 1])

    def fold_ring(r):
        add_to(zrow(part, r, z, 0, HALF), land2z.at[r, 0], land2z.at[r, 1])
        add_to(ycol(part, r, y, HALF, HALF), land2y.at[r, 0], land2y.at[r, 1])

    def fold_corner(r):
        add_to(blk(part, r, z, ym, 0, QUART), land3.at[r, 0])
        add_to(blk(part, r, z, yp, QUART, QUART), land3.at[r, 1])
        add_to(blk(part, r, zm, y, HALF, QUART), land3.at[r, 2])
        add_to(blk(part, r, zp, y, HALF + QUART, QUART), land3.at[r, 3])

    def finish(r):
        for part_no in range(2):
            base = part_no * HALF
            total = blk(cots, r, z, y, base, HALF)[...].astype(F32)
            total = total + blk(part, r, z, y, base, HALF)[...].astype(F32)
            total = total + land4[r, part_no * 2].astype(F32)
            total = total + land4[r, part_no * 2 + 1].astype(F32)
            outs[r, :, base:base + HALF] = total.astype(BF16)
        if r < CHUNKS:
            move(r).start()

    def act(kind, i):
        phase = int(kind[1:]) - 1 if len(kind) > 1 else 4
        if kind[0] == "P":
            if phase == 0:
                row_load(i).wait()
                if i < CHUNKS:
                    cot_load(i).wait()
                else:
                    c = i - CHUNKS
                    move(c).wait_recv()
                    top = sec == n_sec - 1
                    value = jnp.where(top, head[at_rows(c), :], moved[c])
                    blk(cots, i, z, y, 0, D)[...] = value
            else:
                ag_wait(phase - 1, i)
            ag_start(phase, i)
        else:
            if phase > 0:
                rs_wait(phase - 1, i)
                (fold_far, fold_ring, fold_corner, finish)[phase - 1](i)
            if phase < 4:
                rs_start(phase, i)

    stores = [
        pltpu.make_async_copy(wg, grad_gate, load_sem.at[0]),
        pltpu.make_async_copy(wu, grad_up, load_sem.at[1]),
        pltpu.make_async_copy(wd, grad_down, load_sem.at[2]),
        pltpu.make_async_copy(outs, grads, load_sem.at[3]),
    ]

    pl.semaphore_wait(barrier, 6)
    for number, (kind, i) in enumerate(HEAD):
        act(kind, i)
        if number == CHUNKS:
            acc_g[...] = jnp.zeros_like(acc_g)
            acc_u[...] = jnp.zeros_like(acc_u)
            acc_d[...] = jnp.zeros_like(acc_d)
    for copy in loads:
        copy.wait()

    @pl.loop(0, STEPS + 1)
    def _(t):
        def after(step):
            for (when, name), todo in AFTER.items():
                if name == step:
                    @pl.when(t == when)
                    def _():
                        for kind, i in todo:
                            act(kind, i)

        for step, work in (("F", forward), ("G", backward), ("H", send_back)):
            @pl.when(t < STEPS)
            def _():
                if step == "F":
                    ag_wait(3, t)
                work(t)
            after(step)
        for step, work in (("V", grow_up_gate), ("W", grow_down)):
            @pl.when(t > 0)
            def _():
                work(t - 1)
            if step == "W":
                @pl.when(t == STEPS)
                def _():
                    for target, total, copy in zip((wg, wu, wd), (acc_g, acc_u, acc_d), stores):
                        target[...] = total[...].astype(BF16)
                        copy.start()
            after(step)

    stores[3].start()

    @pl.loop(0, STEPS)
    def _(k):
        for phase in range(4):
            for which in range(2):
                for side in range(2):
                    ag_copy(which, phase, side, k, False).wait_send()
                    rs_copy(phase, which, side, k).wait_send()

    @pl.loop(0, CHUNKS)
    def _(c):
        move(c).wait_send()

    for copy in stores:
        copy.wait()


def on_device(inputs, routes, gates, cot_early, head_grad, w_gate, w_up, w_down):
    hbm = pl.BlockSpec(memory_space=pl.ANY)
    vmem = pl.BlockSpec(memory_space=pltpu.VMEM)
    shape = jax.ShapeDtypeStruct
    block = SIDE * ROWS
    grads, grad_gate, grad_up, grad_down = pl.pallas_call(
        kernel,
        out_shape=(
            shape((STEPS, ROWS, D), BF16),
            shape((D, FF), BF16),
            shape((D, FF), BF16),
            shape((FF, D), BF16),
        ),
        in_specs=[hbm, vmem, vmem, hbm, hbm, hbm, hbm, hbm],
        out_specs=[hbm] * 4,
        scratch_shapes=[
            pltpu.VMEM((STEPS, SIDE, block, D), BF16),
            pltpu.VMEM((STEPS, SIDE, block, WIDE), BF16),
            pltpu.VMEM((STEPS, SIDE, block, D), BF16),
            pltpu.VMEM((STEPS, 2, block, QUART), BF16),
            pltpu.VMEM((STEPS, 2, SIDE, ROWS, QUART), BF16),
            pltpu.VMEM((STEPS, 2, block, HALF), BF16),
            pltpu.VMEM((STEPS, 2, SIDE, ROWS, HALF), BF16),
            pltpu.VMEM((STEPS, 4, ROWS, QUART), BF16),
            pltpu.VMEM((STEPS, 4, ROWS, HALF), BF16),
            pltpu.VMEM((CHUNKS, ROWS, D), BF16),
            pltpu.VMEM((STEPS, ROWS, D), BF16),
            pltpu.VMEM((CHUNKS * ROWS, D), BF16),
            pltpu.VMEM((D, FF), BF16),
            pltpu.VMEM((D, FF), BF16),
            pltpu.VMEM((FF, D), BF16),
            pltpu.VMEM((ALL_ROWS, FF), F32),
            pltpu.VMEM((ALL_ROWS, FF), F32),
            pltpu.VMEM((2, ALL_ROWS, FF), BF16),
            pltpu.VMEM((2, ALL_ROWS, FF), BF16),
            pltpu.VMEM((2, ALL_ROWS, FF), BF16),
            pltpu.VMEM((2, ALL_ROWS, D), BF16),
            pltpu.VMEM((D, FF), F32),
            pltpu.VMEM((D, FF), F32),
            pltpu.VMEM((FF, D), F32),
            pltpu.SemaphoreType.DMA((4 + STEPS + CHUNKS,)),
            pltpu.SemaphoreType.DMA((STEPS, 2, 8)),
            pltpu.SemaphoreType.DMA((STEPS, 2, 8)),
            pltpu.SemaphoreType.DMA((STEPS, 16)),
            pltpu.SemaphoreType.DMA((STEPS, 16)),
            pltpu.SemaphoreType.DMA((CHUNKS,)),
            pltpu.SemaphoreType.DMA((CHUNKS,)),
        ],
        compiler_params=pltpu.CompilerParams(
            collective_id=0, has_side_effects=True, vmem_limit_bytes=67043328
        ),
        cost_estimate=pl.CostEstimate(
            flops=16 * 2 * 1024 * D * FF, bytes_accessed=16 << 20, transcendentals=2 * 1024 * FF
        ),
    )(inputs[0], jnp.transpose(routes[0], (2, 0, 1)), jnp.transpose(gates[0], (2, 0, 1)), cot_early[0], head_grad, w_gate[0, 0], w_up[0, 0], w_down[0, 0])
    tokens = CHUNKS * ROWS
    grads = grads.reshape(2, 1, tokens, D)
    return grads[0], grads[1], grad_gate[None, None], grad_up[None, None], grad_down[None, None]


def solution(mesh):
    in_specs = (
        P("section", None, "expert", None),
        P("section", None, "expert", None),
        P("section", None, "expert", None),
        P("section", "expert", None),
        P("expert", None),
        P("section", "expert", None, None),
        P("section", "expert", None, None),
        P("section", "expert", None, None),
    )
    out_specs = (
        P("section", "expert", None),
        P("section", "expert", None),
        P("section", "expert", None, None),
        P("section", "expert", None, None),
        P("section", "expert", None, None),
    )
    return jax.shard_map(
        on_device, mesh=mesh, in_specs=in_specs, out_specs=out_specs, check_vma=False
    )
```

```python
import functools

import jax
import jax.numpy as jnp
from jax import lax
from jax.experimental import pallas as pl
from jax.experimental.pallas import tpu as pltpu
from jax.sharding import PartitionSpec as P

F32 = jnp.float32
BF16 = jnp.bfloat16
MESH = pl.DeviceIdType.MESH

D = 2048
FF = 512
TOPK = 10
OWNERS = 16
SIDE = 4
ROWS = 16
CHUNKS = 4
STEPS = 2 * CHUNKS
WIDE = D + 128
HALF = D // 2
QUART = D // 4
COT_CUT = 1024
ALL_ROWS = OWNERS * ROWS
NT = (((1,), (1,)), ((), ()))
TN = (((0,), (0,)), ((), ()))
HEAD = (("P1", 0), ("P1", 1), ("P1", 2), ("P2", 0), ("P1", 3), ("P2", 1), ("P2", 2), ("P3", 0), ("P2", 3),
        ("P3", 1), ("P4", 0), ("P3", 2), ("P4", 1),)
AFTER = {
    (0, "H"): (("P3", 3), ("P4", 2),),
    (1, "W"): (("R1", 0), ("P4", 3),),
    (2, "G"): (("R1", 1), ("R2", 0),),
    (2, "W"): (("R1", 2),),
    (3, "F"): (("R2", 1),),
    (3, "G"): (("R3", 0),),
    (3, "H"): (("R1", 3), ("R2", 2),),
    (3, "W"): (("R4", 0), ("R3", 1), ("R2", 3), ("R3", 2), ("M", 0), ("R4", 1), ("P1", 4), ("R3", 3), ("R4",
        2), ("M", 1), ("P2", 4), ("R4", 3), ("M", 2), ("P1", 5), ("P3", 4), ("M", 3), ("P2", 5), ("P1", 6),
        ("P1", 7), ("P4", 4), ("P2", 6), ("P3", 5), ("P2", 7),),
    (4, "H"): (("P3", 6),),
    (4, "W"): (("P4", 5), ("P3", 7), ("P4", 6),),
    (5, "W"): (("R1", 4), ("P4", 7),),
    (6, "G"): (("R1", 5), ("R2", 4),),
    (6, "W"): (("R1", 6),),
    (7, "F"): (("R2", 5),),
    (7, "H"): (("R1", 7), ("R2", 6),),
    (8, "V"): (("R2", 7),),
    (8, "W"): (("R3", 4), ("R3", 5), ("R3", 6), ("R3", 7), ("R4", 4), ("R4", 5), ("R4", 6), ("R4", 7), ("M",
        4), ("M", 5), ("M", 6), ("M", 7),),
}


def kernel(
    inputs, routes, gates, cot_early, head_grad, w_gate, w_up, w_down,
    early, late, grad_gate, grad_up, grad_down,
    xs, cots, part, land1z, land1y, land2z, land2y, land3, land4, moved, head,
    wg, wu, wd, gate_s, up_s, hid_s, gg_s, gu_s, scaled_s, acc_g, acc_u, acc_d,
    load_sem, ag_send, ag_recv, rs_send, rs_recv, mv_send, mv_recv,
):
    sec = lax.axis_index("section")
    own = lax.axis_index("expert")
    n_sec = lax.axis_size("section")
    z = own // SIDE
    y = own % SIDE
    zp, zm, zo = (z + 1) % SIDE, (z + 3) % SIDE, (z + 2) % SIDE
    yp, ym, yo = (y + 1) % SIDE, (y + 3) % SIDE, (y + 2) % SIDE
    to_zp = (sec, zp * SIDE + y)
    to_zm = (sec, zm * SIDE + y)
    to_yp = (sec, z * SIDE + yp)
    to_ym = (sec, z * SIDE + ym)
    to_below = ((sec + n_sec - 1) % n_sec, own)
    to_above = ((sec + 1) % n_sec, own)

    def at_rows(i):
        return pl.ds(pl.multiple_of(i * ROWS, ROWS), ROWS)

    def blk(buf, k, bz, by, col, width):
        return buf.at[k, bz, at_rows(by), pl.ds(col, width)]

    def zrow(buf, k, bz, col, width):
        return buf.at[k, bz, :, pl.ds(col, width)]

    def ycol(buf, k, by, col, width):
        return buf.at[k, :, at_rows(by), pl.ds(col, width)]

    def remote(src, dst, send, recv, peer):
        return pltpu.make_async_remote_copy(
            src_ref=src, dst_ref=dst, send_sem=send, recv_sem=recv,
            device_id=peer, device_id_type=MESH,
        )

    def ag_copy(which, phase, side, k, arriving):
        buf = cots if which else xs
        width = WIDE if which else D
        cut = COT_CUT if which else HALF
        late = phase >= 2
        on_y = (phase < 2) != bool(which)
        here, plus, minus = (y, yp, ym) if on_y else (z, zp, zm)
        peer = ((to_yp, to_ym) if on_y else (to_zp, to_zm))[side]
        opposite = yo if on_y else zo
        if phase % 2 == 0:
            pos = ((minus, plus)[side]) if arriving else here
            col, wid = 0, width
        else:
            pos = opposite if arriving else (minus, plus)[side]
            col, wid = (0, cut) if side == 0 else (cut, width - cut)
        if late:
            ref = (ycol if on_y else zrow)(buf, k, pos, col, wid)
        elif on_y:
            ref = blk(buf, k, z, pos, col, wid)
        else:
            ref = blk(buf, k, pos, y, col, wid)
        slot = phase * 2 + side
        return remote(ref, ref, ag_send.at[k, which, slot], ag_recv.at[k, which, slot], peer)

    def ag_start(phase, k):
        for which in range(2):
            for side in range(2):
                ag_copy(which, phase, side, k, False).start()

    def ag_wait(phase, k):
        for which in range(2):
            for side in range(2):
                ag_copy(which, phase, side, k, True).wait_recv()

    def rs_copy(phase, part_no, side, k):
        on_y = (part_no == 1) != (phase >= 2)
        base = part_no * HALF
        plus, minus, opposite = (yp, ym, yo) if on_y else (zp, zm, zo)
        peer = ((to_ym, to_yp) if on_y else (to_zm, to_zp))[side]
        if phase % 2 == 0:
            pos = opposite
            col, wid = base + side * QUART, QUART
        else:
            pos = (minus, plus)[side]
            col, wid = base, HALF
        if phase < 2:
            src = (ycol if on_y else zrow)(part, k, pos, col, wid)
            lands = ((land1z, land2z), (land1y, land2y))[part_no]
            dst = lands[phase].at[k, side]
        else:
            src = blk(part, k, z, pos, col, wid) if on_y else blk(part, k, pos, y, col, wid)
            dst = (land3, land4)[phase - 2].at[k, part_no * 2 + side]
        slot = phase * 4 + part_no * 2 + side
        return remote(src, dst, rs_send.at[k, slot], rs_recv.at[k, slot], peer)

    def rs_start(phase, k):
        for part_no in range(2):
            for side in range(2):
                rs_copy(phase, part_no, side, k).start()

    def rs_wait(phase, k):
        for part_no in range(2):
            for side in range(2):
                rs_copy(phase, part_no, side, k).wait_recv()

    def add_to(ref, *others):
        total = ref[...].astype(F32)
        for other in others:
            total = total + other[...].astype(F32)
        ref[...] = total.astype(BF16)

    def move(c):
        return remote(early.at[c], moved.at[c], mv_send.at[c], mv_recv.at[c], to_below)

    loads = [
        pltpu.make_async_copy(w_gate, wg, load_sem.at[0]),
        pltpu.make_async_copy(w_up, wu, load_sem.at[1]),
        pltpu.make_async_copy(w_down, wd, load_sem.at[2]),
        pltpu.make_async_copy(head_grad, head, load_sem.at[3]),
    ]

    def row_load(k):
        c = k % CHUNKS
        m = k // CHUNKS
        return pltpu.make_async_copy(
            inputs.at[m, pl.ds(c * ROWS, ROWS), :], blk(xs, k, z, y, 0, D), load_sem.at[4 + k]
        )

    def cot_load(c):
        return pltpu.make_async_copy(
            cot_early.at[pl.ds(c * ROWS, ROWS), :], blk(cots, c, z, y, 0, D), load_sem.at[4 + STEPS + c]
        )

    for c in range(CHUNKS):
        row_load(c).start()
        cot_load(c).start()
    for copy in loads:
        copy.start()
    for c in range(CHUNKS, STEPS):
        row_load(c).start()

    barrier = pltpu.get_barrier_semaphore()
    for peer in (to_yp, to_ym, to_zp, to_zm, to_below, to_above):
        pl.semaphore_signal(barrier, inc=1, device_id=peer, device_id_type=MESH)

    expert = lax.broadcasted_iota(jnp.int32, (OWNERS, CHUNKS * ROWS), 0)
    halves = []
    for m in range(2):
        dense = jnp.zeros((OWNERS, CHUNKS * ROWS), F32)
        for choice in range(TOPK):
            hit = routes[choice, m:m + 1, :] == expert
            dense = dense + jnp.where(hit, gates[choice, m:m + 1, :], 0.0)
        halves.append(dense)
    dense = jnp.concatenate(halves, axis=1)
    high = dense.astype(BF16).astype(F32)
    mid = (dense - high).astype(BF16).astype(F32)
    low = dense - high - mid
    blank = jnp.zeros((128 - 3 * OWNERS, STEPS * ROWS), F32)
    packed = jnp.concatenate([high, mid, low, blank], axis=0).T.astype(BF16)
    for k in range(STEPS):
        blk(cots, k, z, y, D, 128)[...] = packed[k * ROWS:(k + 1) * ROWS]

    pick_row = lax.broadcasted_iota(jnp.int32, (128, 128), 0)
    picker = jnp.where(
        ((pick_row & (OWNERS - 1)) == own) & (pick_row < 3 * OWNERS), 1.0, 0.0
    ).astype(BF16)

    def forward(j):
        rows = xs[j].reshape(ALL_ROWS, D)
        for n in range(2):
            cols = slice(n * 256, (n + 1) * 256)
            gate_s[:, cols] = jnp.dot(rows, wg[:, cols], preferred_element_type=F32)
            up_s[:, cols] = jnp.dot(rows, wu[:, cols], preferred_element_type=F32)

    def backward(j):
        turn = j % 2
        own_gate = jnp.dot(
            cots[j, :, :, D:].reshape(ALL_ROWS, 128), picker, preferred_element_type=F32
        )
        for n in range(D // 128):
            cols = slice(n * 128, (n + 1) * 128)
            tile = cots[j, :, :, cols].reshape(ALL_ROWS, 128).astype(F32)
            scaled_s[turn, :, cols] = (own_gate * tile).astype(BF16)
        for n in range(2):
            cols = slice(n * 256, (n + 1) * 256)
            grad_hidden = lax.dot_general(
                scaled_s[turn], wd[cols, :], NT, preferred_element_type=F32
            )
            gate_value = gate_s[:, cols]
            up_value = up_s[:, cols]
            sigmoid_value = jax.nn.sigmoid(gate_value)
            swished = gate_value * sigmoid_value
            derivative = sigmoid_value * (1.0 + gate_value * (1.0 - sigmoid_value))
            hid_s[turn, :, cols] = (swished * up_value).astype(BF16)
            gg_s[turn, :, cols] = (grad_hidden * up_value * derivative).astype(BF16)
            gu_s[turn, :, cols] = (grad_hidden * swished).astype(BF16)
    def send_back(j):
        turn = j % 2
        for n in range(D // 256):
            cols = slice(n * 256, (n + 1) * 256)
            back = lax.dot_general(gg_s[turn], wg[cols, :], NT, preferred_element_type=F32)
            back = back + lax.dot_general(gu_s[turn], wu[cols, :], NT, preferred_element_type=F32)
            part[j, :, :, cols] = back.astype(BF16).reshape(SIDE, SIDE * ROWS, 256)

    def grow_up_gate(r):
        turn = r % 2
        for n in range(D // 256):
            cols = slice(n * 256, (n + 1) * 256)
            rows = xs[r, :, :, cols].reshape(ALL_ROWS, 256)
            acc_g[cols, :] += lax.dot_general(rows, gg_s[turn], TN, preferred_element_type=F32)
            acc_u[cols, :] += lax.dot_general(rows, gu_s[turn], TN, preferred_element_type=F32)

    def grow_down(r):
        turn = r % 2
        for n in range(D // 256):
            cols = slice(n * 256, (n + 1) * 256)
            acc_d[:, cols] += lax.dot_general(
                hid_s[turn], scaled_s[turn, :, cols], TN, preferred_element_type=F32
            )

    def fold_far(r):
        add_to(zrow(part, r, zm, 0, QUART), land1z.at[r, 0])
        add_to(zrow(part, r, zp, QUART, QUART), land1z.at[r, 1])
        add_to(ycol(part, r, ym, HALF, QUART), land1y.at[r, 0])
        add_to(ycol(part, r, yp, HALF + QUART, QUART), land1y.at[r, 1])

    def fold_ring(r):
        add_to(zrow(part, r, z, 0, HALF), land2z.at[r, 0], land2z.at[r, 1])
        add_to(ycol(part, r, y, HALF, HALF), land2y.at[r, 0], land2y.at[r, 1])

    def fold_corner(r):
        add_to(blk(part, r, z, ym, 0, QUART), land3.at[r, 0])
        add_to(blk(part, r, z, yp, QUART, QUART), land3.at[r, 1])
        add_to(blk(part, r, zm, y, HALF, QUART), land3.at[r, 2])
        add_to(blk(part, r, zp, y, HALF + QUART, QUART), land3.at[r, 3])

    def finish(r):
        for part_no in range(2):
            base = part_no * HALF
            total = blk(cots, r, z, y, base, HALF)[...].astype(F32)
            total = total + blk(part, r, z, y, base, HALF)[...].astype(F32)
            total = total + land4[r, part_no * 2].astype(F32)
            total = total + land4[r, part_no * 2 + 1].astype(F32)
            (early, late)[r // CHUNKS][r % CHUNKS, :, base:base + HALF] = total.astype(BF16)
        if r < CHUNKS:
            move(r).start()

    def act(kind, i):
        phase = int(kind[1:]) - 1 if len(kind) > 1 else 4
        if kind[0] == "P":
            if phase == 0:
                row_load(i).wait()
                if i < CHUNKS:
                    cot_load(i).wait()
                else:
                    c = i - CHUNKS
                    move(c).wait_recv()
                    top = sec == n_sec - 1
                    value = jnp.where(top, head[at_rows(c), :], moved[c])
                    blk(cots, i, z, y, 0, D)[...] = value
            else:
                ag_wait(phase - 1, i)
            ag_start(phase, i)
        else:
            if phase > 0:
                rs_wait(phase - 1, i)
                (fold_far, fold_ring, fold_corner, finish)[phase - 1](i)
            if phase < 4:
                rs_start(phase, i)

    pl.semaphore_wait(barrier, 6)
    for number, (kind, i) in enumerate(HEAD):
        act(kind, i)
        if number == CHUNKS:
            acc_g[...] = jnp.zeros_like(acc_g)
            acc_u[...] = jnp.zeros_like(acc_u)
            acc_d[...] = jnp.zeros_like(acc_d)
    for copy in loads:
        copy.wait()

    @pl.loop(0, STEPS + 1)
    def _(t):
        def after(step):
            for (when, name), todo in AFTER.items():
                if name == step:
                    @pl.when(t == when)
                    def _():
                        for kind, i in todo:
                            act(kind, i)

        for step, work in (("F", forward), ("G", backward), ("H", send_back)):
            @pl.when(t < STEPS)
            def _():
                if step == "F":
                    ag_wait(3, t)
                work(t)
            after(step)
        for step, work in (("V", grow_up_gate), ("W", grow_down)):
            @pl.when(t > 0)
            def _():
                work(t - 1)
            if step == "W":
                @pl.when(t == STEPS)
                def _():
                    for target, total in zip((grad_gate, grad_up, grad_down), (acc_g, acc_u, acc_d)):
                        target[...] = total[...].astype(BF16)
            after(step)

    @pl.loop(0, STEPS)
    def _(k):
        for phase in range(4):
            for which in range(2):
                for side in range(2):
                    ag_copy(which, phase, side, k, False).wait_send()
                    rs_copy(phase, which, side, k).wait_send()

    @pl.loop(0, CHUNKS)
    def _(c):
        move(c).wait_send()


def store_results(*refs):
    sources, targets, sem = refs[:5], refs[5:10], refs[10]
    copies = [
        pltpu.make_async_copy(src, dst, sem.at[i]) for i, (src, dst) in enumerate(zip(sources, targets))
    ]
    for copy in copies:
        copy.start()
    for copy in copies:
        copy.wait()


def on_device(inputs, routes, gates, cot_early, head_grad, w_gate, w_up, w_down):
    hbm = pl.BlockSpec(memory_space=pl.ANY)
    vmem = pl.BlockSpec(memory_space=pltpu.VMEM)
    shape = jax.ShapeDtypeStruct
    block = SIDE * ROWS
    early, late, grad_gate, grad_up, grad_down = pl.pallas_call(
        kernel,
        out_shape=(
            pltpu.VMEM((CHUNKS, ROWS, D), BF16),
            pltpu.VMEM((CHUNKS, ROWS, D), BF16),
            pltpu.VMEM((D, FF), BF16),
            pltpu.VMEM((D, FF), BF16),
            pltpu.VMEM((FF, D), BF16),
        ),
        in_specs=[hbm, vmem, vmem, hbm, hbm, hbm, hbm, hbm],
        out_specs=[vmem] * 5,
        scratch_shapes=[
            pltpu.VMEM((STEPS, SIDE, block, D), BF16),
            pltpu.VMEM((STEPS, SIDE, block, WIDE), BF16),
            pltpu.VMEM((STEPS, SIDE, block, D), BF16),
            pltpu.VMEM((STEPS, 2, block, QUART), BF16),
            pltpu.VMEM((STEPS, 2, SIDE, ROWS, QUART), BF16),
            pltpu.VMEM((STEPS, 2, block, HALF), BF16),
            pltpu.VMEM((STEPS, 2, SIDE, ROWS, HALF), BF16),
            pltpu.VMEM((STEPS, 4, ROWS, QUART), BF16),
            pltpu.VMEM((STEPS, 4, ROWS, HALF), BF16),
            pltpu.VMEM((CHUNKS, ROWS, D), BF16),
            pltpu.VMEM((CHUNKS * ROWS, D), BF16),
            pltpu.VMEM((D, FF), BF16),
            pltpu.VMEM((D, FF), BF16),
            pltpu.VMEM((FF, D), BF16),
            pltpu.VMEM((ALL_ROWS, FF), F32),
            pltpu.VMEM((ALL_ROWS, FF), F32),
            pltpu.VMEM((2, ALL_ROWS, FF), BF16),
            pltpu.VMEM((2, ALL_ROWS, FF), BF16),
            pltpu.VMEM((2, ALL_ROWS, FF), BF16),
            pltpu.VMEM((2, ALL_ROWS, D), BF16),
            pltpu.VMEM((D, FF), F32),
            pltpu.VMEM((D, FF), F32),
            pltpu.VMEM((FF, D), F32),
            pltpu.SemaphoreType.DMA((4 + STEPS + CHUNKS,)),
            pltpu.SemaphoreType.DMA((STEPS, 2, 8)),
            pltpu.SemaphoreType.DMA((STEPS, 2, 8)),
            pltpu.SemaphoreType.DMA((STEPS, 16)),
            pltpu.SemaphoreType.DMA((STEPS, 16)),
            pltpu.SemaphoreType.DMA((CHUNKS,)),
            pltpu.SemaphoreType.DMA((CHUNKS,)),
        ],
        compiler_params=pltpu.CompilerParams(
            collective_id=0, has_side_effects=True, vmem_limit_bytes=59500000
        ),
        cost_estimate=pl.CostEstimate(
            flops=16 * 2 * 1024 * D * FF, bytes_accessed=16 << 20, transcendentals=2 * 1024 * FF
        ),
    )(inputs[0], jnp.transpose(routes[0], (2, 0, 1)), jnp.transpose(gates[0], (2, 0, 1)), cot_early[0], head_grad, w_gate[0, 0], w_up[0, 0], w_down[0, 0])
    results = (early, late, grad_gate, grad_up, grad_down)
    early, late, grad_gate, grad_up, grad_down = pl.pallas_call(
        store_results,
        out_shape=tuple(shape(result.shape, BF16) for result in results),
        in_specs=[hbm] * 5,
        out_specs=[hbm] * 5,
        scratch_shapes=[pltpu.SemaphoreType.DMA((5,))],
        compiler_params=pltpu.CompilerParams(vmem_limit_bytes=1 << 20),
    )(*results)
    early = early.reshape(1, CHUNKS * ROWS, D)
    late = late.reshape(1, CHUNKS * ROWS, D)
    return early, late, grad_gate[None, None], grad_up[None, None], grad_down[None, None]


def solution(mesh):
    in_specs = (
        P("section", None, "expert", None),
        P("section", None, "expert", None),
        P("section", None, "expert", None),
        P("section", "expert", None),
        P("expert", None),
        P("section", "expert", None, None),
        P("section", "expert", None, None),
        P("section", "expert", None, None),
    )
    out_specs = (
        P("section", "expert", None),
        P("section", "expert", None),
        P("section", "expert", None, None),
        P("section", "expert", None, None),
        P("section", "expert", None, None),
    )
    return jax.shard_map(
        on_device, mesh=mesh, in_specs=in_specs, out_specs=out_specs, check_vma=False
    )
```

```python
import functools

import jax
import jax.numpy as jnp
from jax import lax
from jax.experimental import pallas as pl
from jax.experimental.pallas import tpu as pltpu
from jax.sharding import PartitionSpec as P

F32 = jnp.float32
BF16 = jnp.bfloat16
MESH = pl.DeviceIdType.MESH

D = 2048
FF = 512
TOPK = 10
OWNERS = 16
SIDE = 4
ROWS = 16
CHUNKS = 4
STEPS = 2 * CHUNKS
HALF = D // 2
QUART = D // 4
SENT = D - D // 16
ALL_ROWS = OWNERS * ROWS
NT = (((1,), (1,)), ((), ()))
TN = (((0,), (0,)), ((), ()))
HEAD = (("C1", 0), ("P1", 2), ("P1", 0), ("Z", 0), ("C2", 0), ("P1", 1), ("P1", 3), ("C3", 0), ("P2", 0),
        ("P2", 1), ("P2", 2), ("P2", 3), ("C4", 0), ("P3", 0), ("P3", 1), ("P4", 0), ("P3", 2), ("C5", 0),
        ("P4", 1),)
AFTER = {
    (0, "F"): (("P3", 3), ("P4", 2),),
    (0, "H"): (("R1", 0),),
    (1, "W"): (("R1", 1), ("P4", 3),),
    (2, "G"): (("R2", 0), ("R2", 1),),
    (3, "F"): (("R3", 0),),
    (3, "G"): (("R1", 2),),
    (3, "H"): (("R1", 3), ("R3", 1), ("R4", 0), ("R2", 2), ("R2", 3), ("R4", 1), ("M", 0), ("R3", 2), ("P1",
        4),),
    (3, "V"): (("R3", 3), ("M", 1), ("R4", 2), ("P2", 4), ("R4", 3), ("P1", 5),),
    (3, "W"): (("P3", 4), ("P2", 5), ("M", 2), ("M", 3), ("P1", 7), ("P1", 6), ("P4", 4), ("P2", 6), ("P3",
        5),),
    (4, "G"): (("P2", 7),),
    (4, "H"): (("P3", 6), ("P4", 5),),
    (4, "W"): (("P3", 7), ("P4", 6),),
    (5, "H"): (("R1", 4),),
    (5, "V"): (("P4", 7), ("R1", 5),),
    (6, "F"): (("R2", 4),),
    (6, "H"): (("R1", 6),),
    (6, "W"): (("R2", 5),),
    (7, "H"): (("R1", 7), ("R2", 6),),
    (8, "V"): (("R2", 7), ("R3", 4), ("R3", 5),),
    (8, "W"): (("R3", 6), ("R3", 7), ("R4", 4), ("R4", 5), ("R4", 6), ("R4", 7), ("M", 4), ("M", 5), ("M", 6),
        ("M", 7),),
}


def kernel(
    inputs, routes_in, gates_in, cot_early, head_grad, w_gate, w_up, w_down,
    early, late, grad_gate, grad_up, grad_down,
    xs, cots, part, land1z, land1y, land2z, land2y, land3, land4, moved, head, routes, gates, shares, own_gate,
    wg, wu, wd, gate_s, up_s, hid_s, gg_s, gu_s, scaled_s, acc_g, acc_u, acc_d,
    load_sem, ag_send, ag_recv, rs_send, rs_recv, mv_send, mv_recv, gate_send, gate_recv,
):
    sec = lax.axis_index("section")
    own = lax.axis_index("expert")
    n_sec = lax.axis_size("section")
    z = own // SIDE
    y = own % SIDE
    zp, zm, zo = (z + 1) % SIDE, (z + 3) % SIDE, (z + 2) % SIDE
    yp, ym, yo = (y + 1) % SIDE, (y + 3) % SIDE, (y + 2) % SIDE
    to_zp = (sec, zp * SIDE + y)
    to_zm = (sec, zm * SIDE + y)
    to_yp = (sec, z * SIDE + yp)
    to_ym = (sec, z * SIDE + ym)
    to_below = ((sec + n_sec - 1) % n_sec, own)
    to_above = ((sec + 1) % n_sec, own)

    def at_rows(i):
        return pl.ds(pl.multiple_of(i * ROWS, ROWS), ROWS)

    def blk(buf, k, bz, by, col, width):
        return buf.at[k, bz, at_rows(by), pl.ds(col, width)]

    def zrow(buf, k, bz, col, width):
        return buf.at[k, bz, :, pl.ds(col, width)]

    def ycol(buf, k, by, col, width):
        return buf.at[k, :, at_rows(by), pl.ds(col, width)]

    def remote(src, dst, send, recv, peer):
        return pltpu.make_async_remote_copy(
            src_ref=src, dst_ref=dst, send_sem=send, recv_sem=recv,
            device_id=peer, device_id_type=MESH,
        )

    def ag_copy(which, phase, side, k, arriving):
        buf = cots if which else xs
        width, cut = D, HALF
        late = phase >= 2
        on_y = (phase < 2) != bool(which)
        here, plus, minus = (y, yp, ym) if on_y else (z, zp, zm)
        peer = ((to_yp, to_ym) if on_y else (to_zp, to_zm))[side]
        opposite = yo if on_y else zo
        if phase % 2 == 0:
            pos = ((minus, plus)[side]) if arriving else here
            col, wid = 0, width
        else:
            pos = opposite if arriving else (minus, plus)[side]
            col, wid = (0, cut) if side == 0 else (cut, width - cut)
        if late:
            ref = (ycol if on_y else zrow)(buf, k, pos, col, wid)
        elif on_y:
            ref = blk(buf, k, z, pos, col, wid)
        else:
            ref = blk(buf, k, pos, y, col, wid)
        return remote(ref, ref, ag_send.at[k], ag_recv.at[k, phase], peer)

    def gate_copy(phase, side, arriving):
        late = phase >= 2
        here, plus, minus, opposite = (z, zp, zm, zo) if late else (y, yp, ym, yo)
        peer = ((to_zp, to_zm) if late else (to_yp, to_ym))[side]
        if phase % 2 == 0:
            pos = (minus, plus)[side] if arriving else here
            line = pl.ds(0, OWNERS)
        else:
            pos = opposite if arriving else (minus, plus)[side]
            line = pl.ds(side * (OWNERS // 2), OWNERS // 2)
        ref = shares.at[pos, :, line] if late else shares.at[z, pos, line]
        return remote(ref, ref, gate_send, gate_recv.at[phase], peer)

    def ag_start(phase, k):
        for which in range(2):
            for side in range(2):
                ag_copy(which, phase, side, k, False).start()

    def await_bytes(ref, sem):
        pltpu.make_async_copy(ref, ref, sem).wait()

    def ag_wait(phase, k):
        whole = (
            xs.at[k, 0], xs.at[k, 0, :, pl.ds(0, HALF)], xs.at[k], xs.at[k, :, :, pl.ds(0, HALF)]
        )[phase]
        await_bytes(whole, ag_recv.at[k, phase])

    def ag_sent(k):
        await_bytes(xs.at[pl.ds(0, 2), :, :, pl.ds(0, SENT)], ag_send.at[k])

    def rs_copy(phase, part_no, side, k):
        on_y = (part_no == 1) != (phase >= 2)
        base = part_no * HALF
        plus, minus, opposite = (yp, ym, yo) if on_y else (zp, zm, zo)
        peer = ((to_ym, to_yp) if on_y else (to_zm, to_zp))[side]
        if phase % 2 == 0:
            pos = opposite
            col, wid = base + side * QUART, QUART
        else:
            pos = (minus, plus)[side]
            col, wid = base, HALF
        if phase < 2:
            src = (ycol if on_y else zrow)(part, k, pos, col, wid)
            lands = ((land1z, land2z), (land1y, land2y))[part_no]
            dst = lands[phase].at[k, side]
        else:
            src = blk(part, k, z, pos, col, wid) if on_y else blk(part, k, pos, y, col, wid)
            dst = (land3, land4)[phase - 2].at[k, part_no * 2 + side]
        return remote(src, dst, rs_send.at[k], rs_recv.at[k, phase], peer)

    def rs_start(phase, k):
        for part_no in range(2):
            for side in range(2):
                rs_copy(phase, part_no, side, k).start()

    def rs_wait(phase, k):
        whole = (
            part.at[k, 0], part.at[k, :, :, pl.ds(0, HALF)],
            part.at[k, 0, pl.ds(0, ROWS)], part.at[k, 0, pl.ds(0, 2 * ROWS)],
        )[phase]
        await_bytes(whole, rs_recv.at[k, phase])

    def rs_sent(k):
        await_bytes(part.at[k, :, :, pl.ds(0, SENT)], rs_send.at[k])

    def gate_wait(phase):
        width = (QUART, QUART // 2, D, HALF)[phase]
        await_bytes(moved.at[0, :, pl.ds(0, width)], gate_recv.at[phase])

    def add_to(ref, *others):
        total = ref[...].astype(F32)
        for other in others:
            total = total + other[...].astype(F32)
        ref[...] = total.astype(BF16)

    def move(c):
        return remote(early.at[c], moved.at[c], mv_send, mv_recv.at[c], to_below)

    loads = [
        pltpu.make_async_copy(w_gate, wg, load_sem.at[0]),
        pltpu.make_async_copy(w_up, wu, load_sem.at[1]),
        pltpu.make_async_copy(w_down, wd, load_sem.at[2]),
        pltpu.make_async_copy(head_grad, head, load_sem.at[3]),
    ]

    gate_loads = [
        pltpu.make_async_copy(routes_in, routes, load_sem.at[4 + STEPS + CHUNKS]),
        pltpu.make_async_copy(gates_in, gates, load_sem.at[5 + STEPS + CHUNKS]),
    ]

    def row_load(k):
        c = k % CHUNKS
        m = k // CHUNKS
        return pltpu.make_async_copy(
            inputs.at[m, pl.ds(c * ROWS, ROWS), :], blk(xs, k, z, y, 0, D), load_sem.at[4 + k]
        )

    def cot_load(c):
        return pltpu.make_async_copy(
            cot_early.at[pl.ds(c * ROWS, ROWS), :], blk(cots, c, z, y, 0, D), load_sem.at[4 + STEPS + c]
        )

    barrier = pltpu.get_barrier_semaphore()
    for peer in (to_yp, to_ym, to_zp, to_zm, to_below, to_above):
        pl.semaphore_signal(barrier, inc=1, device_id=peer, device_id_type=MESH)
    for copy in gate_loads:
        copy.start()
    for c in range(CHUNKS):
        row_load(c).start()
        cot_load(c).start()
    for copy in loads:
        copy.start()
    for c in range(CHUNKS, STEPS):
        row_load(c).start()

    expert = lax.broadcasted_iota(jnp.int32, (OWNERS, CHUNKS * ROWS), 0)

    def pack_gates():
        halves = []
        for m in range(2):
            dense = jnp.zeros((OWNERS, CHUNKS * ROWS), F32)
            for choice in range(TOPK):
                hit = routes[choice, m:m + 1, :] == expert
                dense = dense + jnp.where(hit, gates[choice, m:m + 1, :], 0.0)
            halves.append(dense)
        shares[z, y] = jnp.concatenate(halves, axis=1)

    def unpack_gates():
        mine = lax.broadcasted_iota(jnp.int32, (OWNERS, STEPS * ROWS), 0) == own
        lines = [
            jnp.sum(jnp.where(mine, shares[bz, by], 0.0), axis=0, keepdims=True)
            for bz in range(SIDE) for by in range(SIDE)
        ]
        lines.append(jnp.zeros((128 - OWNERS, STEPS * ROWS), F32))
        columns = jnp.concatenate(lines, axis=0).T
        for k in range(STEPS):
            for source in range(OWNERS):
                column = columns[k * ROWS:(k + 1) * ROWS, source:source + 1]
                own_gate[k, source * ROWS:(source + 1) * ROWS, :] = jnp.broadcast_to(column, (ROWS, 128))

    def forward(j):
        rows = xs[j].reshape(ALL_ROWS, D)
        for n in range(2):
            cols = slice(n * 256, (n + 1) * 256)
            gate_s[:, cols] = jnp.dot(rows, wg[:, cols], preferred_element_type=F32)
            up_s[:, cols] = jnp.dot(rows, wu[:, cols], preferred_element_type=F32)

    def backward(j):
        turn = j % 2
        for n in range(D // 128):
            cols = slice(n * 128, (n + 1) * 128)
            tile = cots[j, :, :, cols].reshape(ALL_ROWS, 128).astype(F32)
            scaled_s[turn, :, cols] = (own_gate[j] * tile).astype(BF16)
        for n in range(2):
            cols = slice(n * 256, (n + 1) * 256)
            grad_hidden = lax.dot_general(
                scaled_s[turn], wd[cols, :], NT, preferred_element_type=F32
            )
            gate_value = gate_s[:, cols]
            up_value = up_s[:, cols]
            sigmoid_value = jax.nn.sigmoid(gate_value)
            swished = gate_value * sigmoid_value
            derivative = sigmoid_value * (1.0 + gate_value * (1.0 - sigmoid_value))
            hid_s[turn, :, cols] = (swished * up_value).astype(BF16)
            gg_s[turn, :, cols] = (grad_hidden * up_value * derivative).astype(BF16)
            gu_s[turn, :, cols] = (grad_hidden * swished).astype(BF16)
    def send_back(j):
        turn = j % 2
        for n in range(D // 256):
            cols = slice(n * 256, (n + 1) * 256)
            back = lax.dot_general(gg_s[turn], wg[cols, :], NT, preferred_element_type=F32)
            back = back + lax.dot_general(gu_s[turn], wu[cols, :], NT, preferred_element_type=F32)
            part[j, :, :, cols] = back.astype(BF16).reshape(SIDE, SIDE * ROWS, 256)

    def grow_up_gate(r):
        turn = r % 2
        for n in range(D // 256):
            cols = slice(n * 256, (n + 1) * 256)
            rows = xs[r, :, :, cols].reshape(ALL_ROWS, 256)
            acc_g[cols, :] += lax.dot_general(rows, gg_s[turn], TN, preferred_element_type=F32)
            acc_u[cols, :] += lax.dot_general(rows, gu_s[turn], TN, preferred_element_type=F32)

    def grow_down(r):
        turn = r % 2
        for n in range(D // 256):
            cols = slice(n * 256, (n + 1) * 256)
            acc_d[:, cols] += lax.dot_general(
                hid_s[turn], scaled_s[turn, :, cols], TN, preferred_element_type=F32
            )

    def fold_far(r):
        add_to(zrow(part, r, zm, 0, QUART), land1z.at[r, 0])
        add_to(zrow(part, r, zp, QUART, QUART), land1z.at[r, 1])
        add_to(ycol(part, r, ym, HALF, QUART), land1y.at[r, 0])
        add_to(ycol(part, r, yp, HALF + QUART, QUART), land1y.at[r, 1])

    def fold_ring(r):
        add_to(zrow(part, r, z, 0, HALF), land2z.at[r, 0], land2z.at[r, 1])
        add_to(ycol(part, r, y, HALF, HALF), land2y.at[r, 0], land2y.at[r, 1])

    def fold_corner(r):
        add_to(blk(part, r, z, ym, 0, QUART), land3.at[r, 0])
        add_to(blk(part, r, z, yp, QUART, QUART), land3.at[r, 1])
        add_to(blk(part, r, zm, y, HALF, QUART), land3.at[r, 2])
        add_to(blk(part, r, zp, y, HALF + QUART, QUART), land3.at[r, 3])

    def finish(r):
        for part_no in range(2):
            base = part_no * HALF
            total = blk(cots, r, z, y, base, HALF)[...].astype(F32)
            total = total + blk(part, r, z, y, base, HALF)[...].astype(F32)
            total = total + land4[r, part_no * 2].astype(F32)
            total = total + land4[r, part_no * 2 + 1].astype(F32)
            (early, late)[r // CHUNKS][r % CHUNKS, :, base:base + HALF] = total.astype(BF16)
        if r < CHUNKS:
            move(r).start()

    def act(kind, i):
        phase = int(kind[1:]) - 1 if len(kind) > 1 else 4
        if kind[0] == "P":
            if phase == 0:
                row_load(i).wait()
                if i < CHUNKS:
                    cot_load(i).wait()
                else:
                    c = i - CHUNKS
                    move(c).wait_recv()
                    top = sec == n_sec - 1
                    value = jnp.where(top, head[at_rows(c), :], moved[c])
                    blk(cots, i, z, y, 0, D)[...] = value
            else:
                ag_wait(phase - 1, i)
            ag_start(phase, i)
        elif kind[0] == "C":
            if phase == 0:
                for copy in gate_loads:
                    copy.wait()
                pack_gates()
            else:
                gate_wait(phase - 1)
            if phase == 4:
                unpack_gates()
            else:
                for side in range(2):
                    gate_copy(phase, side, False).start()
        elif kind[0] == "Z":
            acc_g[...] = jnp.zeros_like(acc_g)
            acc_u[...] = jnp.zeros_like(acc_u)
            acc_d[...] = jnp.zeros_like(acc_d)
        else:
            if phase > 0:
                rs_wait(phase - 1, i)
                (fold_far, fold_ring, fold_corner, finish)[phase - 1](i)
            if phase < 4:
                rs_start(phase, i)
            else:
                rs_sent(i)

    pl.semaphore_wait(barrier, 6)
    for kind, i in HEAD:
        act(kind, i)
    for copy in loads:
        copy.wait()

    @pl.loop(0, STEPS + 1)
    def _(t):
        def after(step):
            for (when, name), todo in AFTER.items():
                if name == step:
                    @pl.when(t == when)
                    def _():
                        for kind, i in todo:
                            act(kind, i)

        for step, work in (("F", forward), ("G", backward), ("H", send_back)):
            @pl.when(t < STEPS)
            def _():
                if step == "F":
                    ag_wait(3, t)
                work(t)
            after(step)
        for step, work in (("V", grow_up_gate), ("W", grow_down)):
            @pl.when(t > 0)
            def _():
                work(t - 1)
                if step == "W":
                    ag_sent(t - 1)
            if step == "W":
                @pl.when(t == STEPS)
                def _():
                    for target, total in zip((grad_gate, grad_up, grad_down), (acc_g, acc_u, acc_d)):
                        target[...] = total[...].astype(BF16)
            after(step)

    await_bytes(moved, mv_send)
    await_bytes(part.at[0, 0, pl.ds(0, 2 * ROWS), pl.ds(0, SENT)], gate_send)


def store_results(*refs):
    sources, targets, sem = refs[:5], refs[5:10], refs[10]
    copies = [
        pltpu.make_async_copy(src, dst, sem.at[i]) for i, (src, dst) in enumerate(zip(sources, targets))
    ]
    for copy in copies:
        copy.start()
    for copy in copies:
        copy.wait()


def on_device(inputs, routes, gates, cot_early, head_grad, w_gate, w_up, w_down):
    hbm = pl.BlockSpec(memory_space=pl.ANY)
    vmem = pl.BlockSpec(memory_space=pltpu.VMEM)
    shape = jax.ShapeDtypeStruct
    block = SIDE * ROWS
    early, late, grad_gate, grad_up, grad_down = pl.pallas_call(
        kernel,
        out_shape=(
            pltpu.VMEM((CHUNKS, ROWS, D), BF16),
            pltpu.VMEM((CHUNKS, ROWS, D), BF16),
            pltpu.VMEM((D, FF), BF16),
            pltpu.VMEM((D, FF), BF16),
            pltpu.VMEM((FF, D), BF16),
        ),
        in_specs=[hbm] * 8,
        out_specs=[vmem] * 5,
        scratch_shapes=[
            pltpu.VMEM((STEPS, SIDE, block, D), BF16),
            pltpu.VMEM((STEPS, SIDE, block, D), BF16),
            pltpu.VMEM((STEPS, SIDE, block, D), BF16),
            pltpu.VMEM((STEPS, 2, block, QUART), BF16),
            pltpu.VMEM((STEPS, 2, SIDE, ROWS, QUART), BF16),
            pltpu.VMEM((STEPS, 2, block, HALF), BF16),
            pltpu.VMEM((STEPS, 2, SIDE, ROWS, HALF), BF16),
            pltpu.VMEM((STEPS, 4, ROWS, QUART), BF16),
            pltpu.VMEM((STEPS, 4, ROWS, HALF), BF16),
            pltpu.VMEM((CHUNKS, ROWS, D), BF16),
            pltpu.VMEM((CHUNKS * ROWS, D), BF16),
            pltpu.VMEM((TOPK, 2, CHUNKS * ROWS), jnp.int32),
            pltpu.VMEM((TOPK, 2, CHUNKS * ROWS), F32),
            pltpu.VMEM((SIDE, SIDE, OWNERS, STEPS * ROWS), F32),
            pltpu.VMEM((STEPS, ALL_ROWS, 128), F32),
            pltpu.VMEM((D, FF), BF16),
            pltpu.VMEM((D, FF), BF16),
            pltpu.VMEM((FF, D), BF16),
            pltpu.VMEM((ALL_ROWS, FF), F32),
            pltpu.VMEM((ALL_ROWS, FF), F32),
            pltpu.VMEM((2, ALL_ROWS, FF), BF16),
            pltpu.VMEM((2, ALL_ROWS, FF), BF16),
            pltpu.VMEM((2, ALL_ROWS, FF), BF16),
            pltpu.VMEM((2, ALL_ROWS, D), BF16),
            pltpu.VMEM((D, FF), F32),
            pltpu.VMEM((D, FF), F32),
            pltpu.VMEM((FF, D), F32),
            pltpu.SemaphoreType.DMA((6 + STEPS + CHUNKS,)),
            pltpu.SemaphoreType.DMA((STEPS,)),
            pltpu.SemaphoreType.DMA((STEPS, 4)),
            pltpu.SemaphoreType.DMA((STEPS,)),
            pltpu.SemaphoreType.DMA((STEPS, 4)),
            pltpu.SemaphoreType.DMA,
            pltpu.SemaphoreType.DMA((CHUNKS,)),
            pltpu.SemaphoreType.DMA,
            pltpu.SemaphoreType.DMA((4,)),
        ],
        compiler_params=pltpu.CompilerParams(
            collective_id=0, has_side_effects=True, vmem_limit_bytes=59500000
        ),
        cost_estimate=pl.CostEstimate(
            flops=16 * 2 * 1024 * D * FF, bytes_accessed=16 << 20, transcendentals=2 * 1024 * FF
        ),
    )(inputs[0], jnp.transpose(routes[0], (2, 0, 1)), jnp.transpose(gates[0], (2, 0, 1)), cot_early[0], head_grad, w_gate[0, 0], w_up[0, 0], w_down[0, 0])
    results = (early, late, grad_gate, grad_up, grad_down)
    early, late, grad_gate, grad_up, grad_down = pl.pallas_call(
        store_results,
        out_shape=tuple(shape(result.shape, BF16) for result in results),
        in_specs=[hbm] * 5,
        out_specs=[hbm] * 5,
        scratch_shapes=[pltpu.SemaphoreType.DMA((5,))],
        compiler_params=pltpu.CompilerParams(vmem_limit_bytes=1 << 20),
    )(*results)
    early = early.reshape(1, CHUNKS * ROWS, D)
    late = late.reshape(1, CHUNKS * ROWS, D)
    return early, late, grad_gate[None, None], grad_up[None, None], grad_down[None, None]


def solution(mesh):
    in_specs = (
        P("section", None, "expert", None),
        P("section", None, "expert", None),
        P("section", None, "expert", None),
        P("section", "expert", None),
        P("expert", None),
        P("section", "expert", None, None),
        P("section", "expert", None, None),
        P("section", "expert", None, None),
    )
    out_specs = (
        P("section", "expert", None),
        P("section", "expert", None),
        P("section", "expert", None, None),
        P("section", "expert", None, None),
        P("section", "expert", None, None),
    )
    return jax.shard_map(
        on_device, mesh=mesh, in_specs=in_specs, out_specs=out_specs, check_vma=False
    )
```

```python
import functools

import jax
import jax.numpy as jnp
from jax import lax
from jax.experimental import pallas as pl
from jax.experimental.pallas import tpu as pltpu
from jax.sharding import PartitionSpec as P

F32 = jnp.float32
BF16 = jnp.bfloat16
MESH = pl.DeviceIdType.MESH

D = 2048
FF = 512
TOPK = 10
OWNERS = 16
SIDE = 4
ROWS = 16
CHUNKS = 4
STEPS = 2 * CHUNKS
HALF = D // 2
QUART = D // 4
SENT = D - D // 16
ALL_ROWS = OWNERS * ROWS
NT = (((1,), (1,)), ((), ()))
TN = (((0,), (0,)), ((), ()))
HEAD = (
    ("C1", 0), ("P1", 2), ("P1", 0), ("P1", 1), ("Z", 0), ("C2", 0), ("P1", 3), ("P2", 0),
    ("C3", 0), ("P2", 1), ("P2", 2), ("P2", 3), ("P3", 0), ("C4", 0), ("P3", 1), ("P4", 0),
    ("P3", 2), ("C5", 0), ("P4", 1),
)
AFTER = {
    (0, "F"): (("P3", 3), ("P4", 2),),
    (0, "H"): (("R1", 0),),
    (1, "W"): (("R1", 1), ("P4", 3),),
    (2, "G"): (("R2", 0), ("R2", 1),),
    (3, "F"): (("R3", 0),),
    (3, "G"): (("R1", 2),),
    (3, "H"): (("R1", 3), ("R3", 1), ("R4", 0), ("R2", 2), ("R2", 3), ("R4", 1), ("M", 0), ("R3", 2), ("P1",
        4),),
    (3, "V"): (("R3", 3), ("M", 1), ("R4", 2), ("P2", 4), ("R4", 3), ("P1", 5),),
    (3, "W"): (("P3", 4), ("P2", 5), ("M", 2), ("M", 3), ("P1", 7), ("P1", 6), ("P4", 4), ("P2", 6), ("P3",
        5),),
    (4, "G"): (("P2", 7),),
    (4, "H"): (("P3", 6), ("P4", 5),),
    (4, "W"): (("P3", 7), ("P4", 6),),
    (5, "H"): (("R1", 4),),
    (5, "V"): (("P4", 7), ("R1", 5),),
    (6, "F"): (("R2", 4),),
    (6, "H"): (("R1", 6),),
    (6, "W"): (("R2", 5),),
    (7, "H"): (("R1", 7), ("R2", 6),),
    (8, "V"): (("R2", 7), ("R3", 4), ("R3", 5),),
    (8, "W"): (("R3", 6), ("R3", 7), ("R4", 4), ("R4", 5), ("R4", 6), ("R4", 7), ("M", 4), ("M", 5), ("M", 6),
        ("M", 7),),
}


def kernel(
    inputs, routes_in, gates_in, cot_early, head_grad, w_gate, w_up, w_down,
    early, late, grad_gate, grad_up, grad_down,
    xs, cots, part, land1z, land1y, land2z, land2y, land3, land4, moved, head, routes, gates, shares, own_gate,
    wg, wu, wd, gate_s, up_s, hid_s, gg_s, gu_s, scaled_s, acc_g, acc_u, acc_d,
    load_sem, ag_send, ag_recv, rs_send, rs_recv, mv_send, mv_recv, gate_send, gate_recv,
):
    sec = lax.axis_index("section")
    own = lax.axis_index("expert")
    n_sec = lax.axis_size("section")
    z = own // SIDE
    y = own % SIDE
    zp, zm, zo = (z + 1) % SIDE, (z + 3) % SIDE, (z + 2) % SIDE
    yp, ym, yo = (y + 1) % SIDE, (y + 3) % SIDE, (y + 2) % SIDE
    to_zp = (sec, zp * SIDE + y)
    to_zm = (sec, zm * SIDE + y)
    to_yp = (sec, z * SIDE + yp)
    to_ym = (sec, z * SIDE + ym)
    to_below = ((sec + n_sec - 1) % n_sec, own)
    to_above = ((sec + 1) % n_sec, own)

    def at_rows(i):
        return pl.ds(pl.multiple_of(i * ROWS, ROWS), ROWS)

    def blk(buf, k, bz, by, col, width):
        return buf.at[k, bz, at_rows(by), pl.ds(col, width)]

    def zrow(buf, k, bz, col, width):
        return buf.at[k, bz, :, pl.ds(col, width)]

    def ycol(buf, k, by, col, width):
        return buf.at[k, :, at_rows(by), pl.ds(col, width)]

    def remote(src, dst, send, recv, peer):
        return pltpu.make_async_remote_copy(
            src_ref=src, dst_ref=dst, send_sem=send, recv_sem=recv,
            device_id=peer, device_id_type=MESH,
        )

    def own_source(which, k):
        rows = pl.ds(k % CHUNKS * ROWS, ROWS)
        return cot_early.at[rows] if which else inputs.at[k // CHUNKS, rows]

    def ag_copy(which, phase, side, k, arriving):
        buf = cots if which else xs
        width, cut = D, HALF
        late = phase >= 2
        on_y = (phase < 2) != bool(which)
        here, plus, minus = (y, yp, ym) if on_y else (z, zp, zm)
        peer = ((to_yp, to_ym) if on_y else (to_zp, to_zm))[side]
        opposite = yo if on_y else zo
        if phase % 2 == 0:
            pos = ((minus, plus)[side]) if arriving else here
            col, wid = 0, width
        else:
            pos = opposite if arriving else (minus, plus)[side]
            col, wid = (0, cut) if side == 0 else (cut, width - cut)
        if late:
            ref = (ycol if on_y else zrow)(buf, k, pos, col, wid)
        elif on_y:
            ref = blk(buf, k, z, pos, col, wid)
        else:
            ref = blk(buf, k, pos, y, col, wid)
        direct = phase == 0 and isinstance(k, int) and k < CHUNKS
        src = own_source(which, k) if direct else ref
        return remote(src, ref, ag_send.at[k], ag_recv.at[k, phase], peer)

    def gate_copy(phase, side, arriving):
        late = phase >= 2
        here, plus, minus, opposite = (z, zp, zm, zo) if late else (y, yp, ym, yo)
        peer = ((to_zp, to_zm) if late else (to_yp, to_ym))[side]
        if phase % 2 == 0:
            pos = (minus, plus)[side] if arriving else here
            line = pl.ds(0, OWNERS)
        else:
            pos = opposite if arriving else (minus, plus)[side]
            line = pl.ds(side * (OWNERS // 2), OWNERS // 2)
        ref = shares.at[pos, :, line] if late else shares.at[z, pos, line]
        return remote(ref, ref, gate_send, gate_recv.at[phase], peer)

    def ag_start(phase, k):
        for which in range(2):
            for side in range(2):
                ag_copy(which, phase, side, k, False).start()

    def await_bytes(ref, sem):
        pltpu.make_async_copy(ref, ref, sem).wait()

    def ag_wait(phase, k):
        whole = (
            xs.at[k, 0], xs.at[k, 0, :, pl.ds(0, HALF)], xs.at[k], xs.at[k, :, :, pl.ds(0, HALF)]
        )[phase]
        await_bytes(whole, ag_recv.at[k, phase])

    def ag_sent(k):
        await_bytes(xs.at[pl.ds(0, 2), :, :, pl.ds(0, SENT)], ag_send.at[k])

    def rs_copy(phase, part_no, side, k):
        on_y = (part_no == 1) != (phase >= 2)
        base = part_no * HALF
        plus, minus, opposite = (yp, ym, yo) if on_y else (zp, zm, zo)
        peer = ((to_ym, to_yp) if on_y else (to_zm, to_zp))[side]
        if phase % 2 == 0:
            pos = opposite
            col, wid = base + side * QUART, QUART
        else:
            pos = (minus, plus)[side]
            col, wid = base, HALF
        if phase < 2:
            src = (ycol if on_y else zrow)(part, k, pos, col, wid)
            lands = ((land1z, land2z), (land1y, land2y))[part_no]
            dst = lands[phase].at[k, side]
        else:
            src = blk(part, k, z, pos, col, wid) if on_y else blk(part, k, pos, y, col, wid)
            dst = (land3, land4)[phase - 2].at[k, part_no * 2 + side]
        return remote(src, dst, rs_send.at[k], rs_recv.at[k, phase], peer)

    def rs_start(phase, k):
        for part_no in range(2):
            for side in range(2):
                rs_copy(phase, part_no, side, k).start()

    def rs_wait(phase, k):
        whole = (
            part.at[k, 0], part.at[k, :, :, pl.ds(0, HALF)],
            part.at[k, 0, pl.ds(0, ROWS)], part.at[k, 0, pl.ds(0, 2 * ROWS)],
        )[phase]
        await_bytes(whole, rs_recv.at[k, phase])

    def rs_sent(k):
        await_bytes(part.at[k, :, :, pl.ds(0, SENT)], rs_send.at[k])

    def gate_wait(phase):
        width = (QUART, QUART // 2, D, HALF)[phase]
        await_bytes(moved.at[0, :, pl.ds(0, width)], gate_recv.at[phase])

    def add_to(ref, *others):
        total = ref[...].astype(F32)
        for other in others:
            total = total + other[...].astype(F32)
        ref[...] = total.astype(BF16)

    def move(c):
        return remote(early.at[c], moved.at[c], mv_send, mv_recv.at[c], to_below)

    loads = [
        pltpu.make_async_copy(w_gate, wg, load_sem.at[0]),
        pltpu.make_async_copy(w_up, wu, load_sem.at[1]),
        pltpu.make_async_copy(w_down, wd, load_sem.at[2]),
        pltpu.make_async_copy(head_grad, head, load_sem.at[3]),
    ]

    gate_loads = [
        pltpu.make_async_copy(routes_in, routes, load_sem.at[4 + STEPS + CHUNKS]),
        pltpu.make_async_copy(gates_in, gates, load_sem.at[5 + STEPS + CHUNKS]),
    ]

    def row_load(k):
        return pltpu.make_async_copy(own_source(0, k), blk(xs, k, z, y, 0, D), load_sem.at[4 + k])

    def cot_load(c):
        return pltpu.make_async_copy(
            own_source(1, c), blk(cots, c, z, y, 0, D), load_sem.at[4 + STEPS + c]
        )

    barrier = pltpu.get_barrier_semaphore()
    for peer in (to_yp, to_ym, to_zp, to_zm, to_below, to_above):
        pl.semaphore_signal(barrier, inc=1, device_id=peer, device_id_type=MESH)
    for copy in gate_loads:
        copy.start()
    for c in range(CHUNKS):
        row_load(c).start()
        cot_load(c).start()
    for copy in loads:
        copy.start()
    for c in range(CHUNKS, STEPS):
        row_load(c).start()

    expert = lax.broadcasted_iota(jnp.int32, (OWNERS, CHUNKS * ROWS), 0)

    def pack_gates():
        halves = []
        for m in range(2):
            dense = jnp.zeros((OWNERS, CHUNKS * ROWS), F32)
            for choice in range(TOPK):
                hit = routes[choice, m:m + 1, :] == expert
                dense = dense + jnp.where(hit, gates[choice, m:m + 1, :], 0.0)
            halves.append(dense)
        shares[z, y] = jnp.concatenate(halves, axis=1)

    def unpack_gates():
        mine = lax.broadcasted_iota(jnp.int32, (OWNERS, STEPS * ROWS), 0) == own
        lines = [
            jnp.sum(jnp.where(mine, shares[bz, by], 0.0), axis=0, keepdims=True)
            for bz in range(SIDE) for by in range(SIDE)
        ]
        lines.append(jnp.zeros((128 - OWNERS, STEPS * ROWS), F32))
        columns = jnp.concatenate(lines, axis=0).T
        for k in range(STEPS):
            for source in range(OWNERS):
                column = columns[k * ROWS:(k + 1) * ROWS, source:source + 1]
                own_gate[k, source * ROWS:(source + 1) * ROWS, :] = jnp.broadcast_to(column, (ROWS, 128))

    def forward(j):
        rows = xs[j].reshape(ALL_ROWS, D)
        for n in range(2):
            cols = slice(n * 256, (n + 1) * 256)
            gate_s[:, cols] = jnp.dot(rows, wg[:, cols], preferred_element_type=F32)
            up_s[:, cols] = jnp.dot(rows, wu[:, cols], preferred_element_type=F32)

    def backward(j):
        turn = j % 2
        for n in range(D // 128):
            cols = slice(n * 128, (n + 1) * 128)
            tile = cots[j, :, :, cols].reshape(ALL_ROWS, 128).astype(F32)
            scaled_s[turn, :, cols] = (own_gate[j] * tile).astype(BF16)
        for n in range(2):
            cols = slice(n * 256, (n + 1) * 256)
            grad_hidden = lax.dot_general(
                scaled_s[turn], wd[cols, :], NT, preferred_element_type=F32
            )
            gate_value = gate_s[:, cols]
            up_value = up_s[:, cols]
            sigmoid_value = jax.nn.sigmoid(gate_value)
            swished = gate_value * sigmoid_value
            derivative = sigmoid_value * (1.0 + gate_value * (1.0 - sigmoid_value))
            hid_s[turn, :, cols] = (swished * up_value).astype(BF16)
            gg_s[turn, :, cols] = (grad_hidden * up_value * derivative).astype(BF16)
            gu_s[turn, :, cols] = (grad_hidden * swished).astype(BF16)
    def send_back(j):
        turn = j % 2
        for n in range(D // 256):
            cols = slice(n * 256, (n + 1) * 256)
            back = lax.dot_general(gg_s[turn], wg[cols, :], NT, preferred_element_type=F32)
            back = back + lax.dot_general(gu_s[turn], wu[cols, :], NT, preferred_element_type=F32)
            part[j, :, :, cols] = back.astype(BF16).reshape(SIDE, SIDE * ROWS, 256)

    def grow_up_gate(r):
        turn = r % 2
        for n in range(D // 256):
            cols = slice(n * 256, (n + 1) * 256)
            rows = xs[r, :, :, cols].reshape(ALL_ROWS, 256)
            acc_g[cols, :] += lax.dot_general(rows, gg_s[turn], TN, preferred_element_type=F32)
            acc_u[cols, :] += lax.dot_general(rows, gu_s[turn], TN, preferred_element_type=F32)

    def grow_down(r):
        turn = r % 2
        for n in range(D // 256):
            cols = slice(n * 256, (n + 1) * 256)
            acc_d[:, cols] += lax.dot_general(
                hid_s[turn], scaled_s[turn, :, cols], TN, preferred_element_type=F32
            )

    def fold_far(r):
        add_to(zrow(part, r, zm, 0, QUART), land1z.at[r, 0])
        add_to(zrow(part, r, zp, QUART, QUART), land1z.at[r, 1])
        add_to(ycol(part, r, ym, HALF, QUART), land1y.at[r, 0])
        add_to(ycol(part, r, yp, HALF + QUART, QUART), land1y.at[r, 1])

    def fold_ring(r):
        add_to(zrow(part, r, z, 0, HALF), land2z.at[r, 0], land2z.at[r, 1])
        add_to(ycol(part, r, y, HALF, HALF), land2y.at[r, 0], land2y.at[r, 1])

    def fold_corner(r):
        add_to(blk(part, r, z, ym, 0, QUART), land3.at[r, 0])
        add_to(blk(part, r, z, yp, QUART, QUART), land3.at[r, 1])
        add_to(blk(part, r, zm, y, HALF, QUART), land3.at[r, 2])
        add_to(blk(part, r, zp, y, HALF + QUART, QUART), land3.at[r, 3])

    def finish(r):
        for part_no in range(2):
            base = part_no * HALF
            total = blk(cots, r, z, y, base, HALF)[...].astype(F32)
            total = total + blk(part, r, z, y, base, HALF)[...].astype(F32)
            total = total + land4[r, part_no * 2].astype(F32)
            total = total + land4[r, part_no * 2 + 1].astype(F32)
            (early, late)[r // CHUNKS][r % CHUNKS, :, base:base + HALF] = total.astype(BF16)
        if r < CHUNKS:
            move(r).start()

    def act(kind, i):
        phase = int(kind[1:]) - 1 if len(kind) > 1 else 4
        if kind[0] == "P":
            if phase == 0:
                if i >= CHUNKS:
                    row_load(i).wait()
                    c = i - CHUNKS
                    move(c).wait_recv()
                    top = sec == n_sec - 1
                    value = jnp.where(top, head[at_rows(c), :], moved[c])
                    blk(cots, i, z, y, 0, D)[...] = value
            else:
                if phase == 2 and i < CHUNKS:
                    row_load(i).wait()
                    cot_load(i).wait()
                ag_wait(phase - 1, i)
            ag_start(phase, i)
        elif kind[0] == "C":
            if phase == 0:
                for copy in gate_loads:
                    copy.wait()
                pack_gates()
            else:
                gate_wait(phase - 1)
            if phase == 4:
                unpack_gates()
            else:
                for side in range(2):
                    gate_copy(phase, side, False).start()
        elif kind[0] == "Z":
            acc_g[...] = jnp.zeros_like(acc_g)
            acc_u[...] = jnp.zeros_like(acc_u)
            acc_d[...] = jnp.zeros_like(acc_d)
        else:
            if phase > 0:
                rs_wait(phase - 1, i)
                (fold_far, fold_ring, fold_corner, finish)[phase - 1](i)
            if phase < 4:
                rs_start(phase, i)
            else:
                rs_sent(i)

    pl.semaphore_wait(barrier, 6)
    for kind, i in HEAD:
        act(kind, i)
    for copy in loads:
        copy.wait()

    @pl.loop(0, STEPS + 1)
    def _(t):
        def after(step):
            for (when, name), todo in AFTER.items():
                if name == step:
                    @pl.when(t == when)
                    def _():
                        for kind, i in todo:
                            act(kind, i)

        for step, work in (("F", forward), ("G", backward), ("H", send_back)):
            @pl.when(t < STEPS)
            def _():
                if step == "F":
                    ag_wait(3, t)
                work(t)
            after(step)
        for step, work in (("V", grow_up_gate), ("W", grow_down)):
            @pl.when(t > 0)
            def _():
                work(t - 1)
                if step == "W":
                    ag_sent(t - 1)
            if step == "W":
                @pl.when(t == STEPS)
                def _():
                    for target, total in zip((grad_gate, grad_up, grad_down), (acc_g, acc_u, acc_d)):
                        target[...] = total[...].astype(BF16)
            after(step)

    await_bytes(moved, mv_send)
    await_bytes(part.at[0, 0, pl.ds(0, 2 * ROWS), pl.ds(0, SENT)], gate_send)


def store_results(*refs):
    sources, targets, sem = refs[:5], refs[5:10], refs[10]
    copies = [
        pltpu.make_async_copy(src, dst, sem.at[i]) for i, (src, dst) in enumerate(zip(sources, targets))
    ]
    for copy in copies:
        copy.start()
    for copy in copies:
        copy.wait()


def on_device(inputs, routes, gates, cot_early, head_grad, w_gate, w_up, w_down):
    hbm = pl.BlockSpec(memory_space=pl.ANY)
    vmem = pl.BlockSpec(memory_space=pltpu.VMEM)
    shape = jax.ShapeDtypeStruct
    block = SIDE * ROWS
    early, late, grad_gate, grad_up, grad_down = pl.pallas_call(
        kernel,
        out_shape=(
            pltpu.VMEM((CHUNKS, ROWS, D), BF16),
            pltpu.VMEM((CHUNKS, ROWS, D), BF16),
            pltpu.VMEM((D, FF), BF16),
            pltpu.VMEM((D, FF), BF16),
            pltpu.VMEM((FF, D), BF16),
        ),
        in_specs=[hbm] * 8,
        out_specs=[vmem] * 5,
        scratch_shapes=[
            pltpu.VMEM((STEPS, SIDE, block, D), BF16),
            pltpu.VMEM((STEPS, SIDE, block, D), BF16),
            pltpu.VMEM((STEPS, SIDE, block, D), BF16),
            pltpu.VMEM((STEPS, 2, block, QUART), BF16),
            pltpu.VMEM((STEPS, 2, SIDE, ROWS, QUART), BF16),
            pltpu.VMEM((STEPS, 2, block, HALF), BF16),
            pltpu.VMEM((STEPS, 2, SIDE, ROWS, HALF), BF16),
            pltpu.VMEM((STEPS, 4, ROWS, QUART), BF16),
            pltpu.VMEM((STEPS, 4, ROWS, HALF), BF16),
            pltpu.VMEM((CHUNKS, ROWS, D), BF16),
            pltpu.VMEM((CHUNKS * ROWS, D), BF16),
            pltpu.VMEM((TOPK, 2, CHUNKS * ROWS), jnp.int32),
            pltpu.VMEM((TOPK, 2, CHUNKS * ROWS), F32),
            pltpu.VMEM((SIDE, SIDE, OWNERS, STEPS * ROWS), F32),
            pltpu.VMEM((STEPS, ALL_ROWS, 128), F32),
            pltpu.VMEM((D, FF), BF16),
            pltpu.VMEM((D, FF), BF16),
            pltpu.VMEM((FF, D), BF16),
            pltpu.VMEM((ALL_ROWS, FF), F32),
            pltpu.VMEM((ALL_ROWS, FF), F32),
            pltpu.VMEM((2, ALL_ROWS, FF), BF16),
            pltpu.VMEM((2, ALL_ROWS, FF), BF16),
            pltpu.VMEM((2, ALL_ROWS, FF), BF16),
            pltpu.VMEM((2, ALL_ROWS, D), BF16),
            pltpu.VMEM((D, FF), F32),
            pltpu.VMEM((D, FF), F32),
            pltpu.VMEM((FF, D), F32),
            pltpu.SemaphoreType.DMA((6 + STEPS + CHUNKS,)),
            pltpu.SemaphoreType.DMA((STEPS,)),
            pltpu.SemaphoreType.DMA((STEPS, 4)),
            pltpu.SemaphoreType.DMA((STEPS,)),
            pltpu.SemaphoreType.DMA((STEPS, 4)),
            pltpu.SemaphoreType.DMA,
            pltpu.SemaphoreType.DMA((CHUNKS,)),
            pltpu.SemaphoreType.DMA,
            pltpu.SemaphoreType.DMA((4,)),
        ],
        compiler_params=pltpu.CompilerParams(
            collective_id=0, has_side_effects=True, vmem_limit_bytes=59500000
        ),
        cost_estimate=pl.CostEstimate(
            flops=16 * 2 * 1024 * D * FF, bytes_accessed=16 << 20, transcendentals=2 * 1024 * FF
        ),
    )(inputs[0], jnp.transpose(routes[0], (2, 0, 1)), jnp.transpose(gates[0], (2, 0, 1)), cot_early[0], head_grad, w_gate[0, 0], w_up[0, 0], w_down[0, 0])
    results = (early, late, grad_gate, grad_up, grad_down)
    early, late, grad_gate, grad_up, grad_down = pl.pallas_call(
        store_results,
        out_shape=tuple(shape(result.shape, BF16) for result in results),
        in_specs=[hbm] * 5,
        out_specs=[hbm] * 5,
        scratch_shapes=[pltpu.SemaphoreType.DMA((5,))],
        compiler_params=pltpu.CompilerParams(vmem_limit_bytes=1 << 20),
    )(*results)
    early = early.reshape(1, CHUNKS * ROWS, D)
    late = late.reshape(1, CHUNKS * ROWS, D)
    return early, late, grad_gate[None, None], grad_up[None, None], grad_down[None, None]


def solution(mesh):
    in_specs = (
        P("section", None, "expert", None),
        P("section", None, "expert", None),
        P("section", None, "expert", None),
        P("section", "expert", None),
        P("expert", None),
        P("section", "expert", None, None),
        P("section", "expert", None, None),
        P("section", "expert", None, None),
    )
    out_specs = (
        P("section", "expert", None),
        P("section", "expert", None),
        P("section", "expert", None, None),
        P("section", "expert", None, None),
        P("section", "expert", None, None),
    )
    return jax.shard_map(
        on_device, mesh=mesh, in_specs=in_specs, out_specs=out_specs, check_vma=False
    )
```
